32 devices in a mesh: slide: 4 (over z), seq: 8 (over y, x, core).
Axes of the slice: x: 2, y: 2, z: 4, core: 2. Of those that a mesh axis runs over, the one named last changes fastest.
Arguments:
- queries: bfloat16 [4096, 2048], P(('slide', 'seq')), parts along dimension 0, may hold values from -10 to 10
- keys: bfloat16 [4096, 2048], P(('slide', 'seq')), parts along dimension 0, may hold values from -6 to 6
- values: bfloat16 [4096, 2048], P(('slide', 'seq')), parts along dimension 0, may hold values from -6 to 6
- out_grad: bfloat16 [4096, 2048], P(('slide', 'seq')), parts along dimension 0, may hold values from -6 to 6
- tissue: int32 [64], P(('slide', 'seq')), parts along dimension 0, may hold values 0 or 1
- valid_count: int32 [4], P('slide'), parts along dimension 0, may hold values from 512 to 1024
Outputs:
- grad_queries: bfloat16 [4096, 2048], P(('slide', 'seq')), parts along dimension 0
- grad_keys: bfloat16 [4096, 2048], P(('slide', 'seq')), parts along dimension 0
- grad_values: bfloat16 [4096, 2048], P(('slide', 'seq')), parts along dimension 0
The draws below stay inside these ranges and needn't reach their ends.
There are 4 independent parts, one for each index of `slide`. The reference program is written for one: setup_inputs(seed, part) draws one part's arguments, and reference() takes and returns one part's arrays. A program takes and returns all parts, laid end to end along the dimension named above; each array names one. Nothing has to cross between parts.
All inputs are finite; a program needn't handle non-finite values. No bound on the sum of `tissue` on one device may be relied on, other than what follows from the above.
Results may differ from the reference program's by a relative error of at most 0.0077.
Values may be sent and summed in bfloat16 or wider, within the bound.
A program may use at most 64 MiB of HBM per device.

```python
import math
import jax
import jax.numpy as jnp
from jax import lax

HEAD_COUNT = 32
HD = 64
D = 2048
SEG = 1024
DILATION_STEP = 8
BLOCK = 64
TILES = 1024
NBLK = 16


def draw_queries(key, part):
    base = jnp.clip(jax.random.normal(jax.random.fold_in(key, 11), (TILES, D), jnp.float32), -6.0, 6.0)
    return base.astype(jnp.bfloat16)


def draw_keys(key, part):
    base = jnp.clip(jax.random.normal(jax.random.fold_in(key, 12), (TILES, D), jnp.float32), -6.0, 6.0)
    return base.astype(jnp.bfloat16)


def set_ends(entries, rng, smallest, top_value):
    longest = entries.shape.index(max(entries.shape))
    spots = []
    for shift in (0, 1):
        where = [jax.random.randint(jax.random.fold_in(rng, axis), (), 0, length) for axis, length in enumerate(entries.shape)]
        where[longest] = (where[longest] + shift) % entries.shape[longest]
        spots.append(tuple(where))
    return entries.at[spots[0]].set(smallest).at[spots[1]].set(top_value)


def levels(rng, shape, split, least, high):
    gain, own = 1.0, jax.random.fold_in(rng, 6)
    for position, shards_of in split:
        steps = jnp.exp(jax.random.uniform(jax.random.fold_in(own, position), (shards_of,), jnp.float32, least / len(split), high / len(split)))
        gain = gain * jnp.repeat(steps, shape[position] // shards_of).reshape([-1 if axis == position else 1 for axis in range(len(shape))])
    return gain


def noise(rng, extent, deviation, reach, cuts=(), kind=jnp.bfloat16):
    drawn = jax.random.normal(rng, extent, jnp.float32) * deviation
    if len(cuts) > 0:
        drawn = levels(rng, extent, cuts, -0.22, 0.18) * drawn
    return jnp.clip(drawn, min=-reach, max=reach).astype(kind)


def setup_inputs(seed: int = 0, part: int = 0) -> dict:
    seeds = jax.random.split(jax.random.key(seed), 7)
    own_keys = jax.random.split(jax.random.fold_in(seeds[6], part), 7)
    queries = draw_queries(jax.random.fold_in(jax.random.fold_in(seeds[6], part), 71), part)
    keys = draw_keys(jax.random.fold_in(jax.random.fold_in(seeds[6], part), 71), part)
    values = noise(own_keys[2], (TILES, D), 1.0, 6.0, ((0, 8),))
    out_grad = noise(own_keys[3], (TILES, D), 1.0, 6.0, ((0, 8),))
    tissue = set_ends((jax.random.randint(own_keys[4], (NBLK,), 0, 4) < 3).astype(jnp.int32), jax.random.fold_in(own_keys[4], 1), 0, 1)
    valid_count = jax.random.randint(own_keys[5], (1,), TILES // 2, TILES + 1).astype(jnp.int32)
    return {"queries": queries, "keys": keys, "values": values, "out_grad": out_grad, "tissue": tissue, "valid_count": valid_count}


NEG = -1e+30

def rounded_copy(input_matrix):
    return lax.optimization_barrier(input_matrix.astype(jnp.bfloat16)).astype(jnp.float32)

def ref_stats(query_rows, key_rows, value_rows, usable, scaling):
    scores = jnp.einsum('...qd,...kd->...qk', query_rows.astype(jnp.float32), key_rows.astype(jnp.float32)) * scaling
    allowed = usable[..., :, None] & usable[..., None, :]
    row_max = lax.optimization_barrier(jnp.max(jnp.where(allowed, scores, NEG), axis=-1))
    weights = jnp.where(allowed, jnp.exp(scores - row_max[..., None]), 0.0)
    totals = lax.optimization_barrier(jnp.sum(weights, axis=-1))
    summed = jnp.einsum('...qk,...kd->...qd', rounded_copy(weights), value_rows.astype(jnp.float32))
    return (row_max, totals, summed)

def ref_grads(query_rows, key_rows, value_rows, grad_rows, usable, log_norm, row_delta, scaling):
    scores = jnp.einsum('...qd,...kd->...qk', query_rows.astype(jnp.float32), key_rows.astype(jnp.float32)) * scaling
    allowed = usable[..., :, None] & usable[..., None, :]
    probs = jnp.where(allowed, jnp.exp(scores - log_norm[..., None]), 0.0)
    grad_value = jnp.einsum('...qk,...qd->...kd', rounded_copy(probs), grad_rows.astype(jnp.float32))
    grad_probs = jnp.einsum('...qd,...kd->...qk', grad_rows.astype(jnp.float32), value_rows.astype(jnp.float32))
    grad_scores = rounded_copy(probs * (grad_probs - row_delta[..., None]))
    grad_query = jnp.einsum('...qk,...kd->...qd', grad_scores, key_rows.astype(jnp.float32)) * scaling
    grad_key = jnp.einsum('...qk,...qd->...kd', grad_scores, query_rows.astype(jnp.float32)) * scaling
    return (grad_query, grad_key, grad_value)

def select_rows(input_matrix, start_shift):
    reshaped_tensor = input_matrix.reshape((input_matrix.shape[0] // DILATION_STEP, DILATION_STEP) + input_matrix.shape[1:])
    return lax.dynamic_index_in_dim(reshaped_tensor, start_shift, axis=1, keepdims=False)

def spread_rows(input_matrix, start_shift, filler):
    picked_index = jnp.arange(DILATION_STEP, dtype=jnp.int32) == start_shift
    return jnp.where(picked_index[None, :], input_matrix[:, None], filler).reshape(-1)

def spread_cols(input_matrix, start_shift, filler):
    picked_index = jnp.arange(DILATION_STEP, dtype=jnp.int32) == start_shift
    return jnp.where(picked_index[None, :, None], input_matrix[:, None, :], filler).reshape(-1, input_matrix.shape[1])

def head_terms(query, key, value, grad, usable, start_shift, scaling):
    seq_rows = query.shape[0]
    segments = seq_rows // SEG

    def by_segment(input_matrix):
        return input_matrix.reshape((segments, SEG) + input_matrix.shape[1:])
    max_w, sum_w, acc_w = ref_stats(by_segment(query), by_segment(key), by_segment(value), by_segment(usable), scaling)
    max_w = max_w.reshape(seq_rows)
    sum_w = sum_w.reshape(seq_rows)
    acc_w = acc_w.reshape(seq_rows, HD)
    usable_d = select_rows(usable, start_shift)
    max_d, sum_d, acc_d = ref_stats(select_rows(query, start_shift), select_rows(key, start_shift), select_rows(value, start_shift), usable_d, scaling)
    max_d = spread_rows(max_d, start_shift, NEG)
    sum_d = spread_rows(sum_d, start_shift, 0.0)
    acc_d = spread_cols(acc_d, start_shift, 0.0)
    largest = jnp.maximum(max_w, max_d)
    totals = sum_w * jnp.exp(max_w - largest) + sum_d * jnp.exp(max_d - largest)
    log_norm = jnp.where(usable, largest + jnp.log(jnp.where(usable, totals, 1.0)), 0.0)
    attended = jnp.exp(max_w - log_norm)[:, None] * acc_w + jnp.exp(max_d - log_norm)[:, None] * acc_d
    row_delta = lax.optimization_barrier(jnp.sum(grad.astype(jnp.float32) * attended, axis=1))
    window = ref_grads(by_segment(query), by_segment(key), by_segment(value), by_segment(grad), by_segment(usable), by_segment(log_norm), by_segment(row_delta), scaling)
    dilated = ref_grads(select_rows(query, start_shift), select_rows(key, start_shift), select_rows(value, start_shift), select_rows(grad, start_shift), usable_d, select_rows(log_norm, start_shift), select_rows(row_delta, start_shift), scaling)
    return tuple((first.reshape(seq_rows, HD) + spread_cols(second, start_shift, 0.0) for first, second in zip(window, dilated)))

def reference(queries, keys, values, out_grad, tissue, valid_count):
    seq_rows = queries.shape[0]
    row_index = jnp.arange(seq_rows, dtype=jnp.int32)
    usable = (row_index < valid_count[0]) & (jnp.repeat(tissue, BLOCK) == 1)
    scaling = 1.0 / math.sqrt(HD)

    def split_heads(input_matrix):
        return input_matrix.reshape(seq_rows, HEAD_COUNT, HD).transpose(1, 0, 2)
    start_shifts = jnp.arange(HEAD_COUNT, dtype=jnp.int32) % DILATION_STEP

    def one_head(pieces):
        return head_terms(pieces[0], pieces[1], pieces[2], pieces[3], usable, pieces[4], scaling)
    grad_query, grad_key, grad_value = lax.map(one_head, (split_heads(queries), split_heads(keys), split_heads(values), split_heads(out_grad), start_shifts))

    def merge_heads(input_matrix):
        return input_matrix.transpose(1, 0, 2).reshape(seq_rows, HEAD_COUNT * HD).astype(jnp.bfloat16)
    return (merge_heads(grad_query), merge_heads(grad_key), merge_heads(grad_value))
```

```python
import functools
import math

import jax
import jax.numpy as jnp
import numpy as np
from jax import lax
from jax.experimental import pallas as pl
from jax.experimental.pallas import tpu as pltpu
from jax.sharding import PartitionSpec as P

HD = 64
SEG = 1024
DILATION_STEP = 8


NEG = -1e30


def dense(input_matrix):
    return input_matrix.reshape(
        input_matrix.shape[0] // DILATION_STEP, DILATION_STEP * input_matrix.shape[1]
    )


def block_stats(query_rows, key_rows, value_rows, usable, scaling):
    scores = (
        jnp.einsum("qd,kd->qk", query_rows, key_rows, preferred_element_type=jnp.float32) * scaling
    )
    allowed = usable[:, None] & usable[None, :]
    row_max = jnp.max(jnp.where(allowed, scores, NEG), axis=1)
    weights = jnp.where(allowed, jnp.exp(scores - row_max[:, None]), 0.0)
    totals = jnp.sum(weights, axis=1)
    summed = jnp.einsum(
        "qk,kd->qd", weights.astype(jnp.bfloat16), value_rows, preferred_element_type=jnp.float32
    )
    return (row_max, totals, summed)


def block_grads(query_rows, key_rows, value_rows, grad_rows, usable, log_norm, row_delta, scaling):
    scores = (
        jnp.einsum("qd,kd->qk", query_rows, key_rows, preferred_element_type=jnp.float32) * scaling
    )
    allowed = usable[:, None] & usable[None, :]
    probs = jnp.where(allowed, jnp.exp(scores - log_norm[:, None]), 0.0)
    results = ()
    results = results + (
        jnp.einsum(
            "qk,qd->kd", probs.astype(jnp.bfloat16), grad_rows, preferred_element_type=jnp.float32
        ),
    )
    grad_probs = jnp.einsum("qd,kd->qk", grad_rows, value_rows, preferred_element_type=jnp.float32)
    grad_scores = (probs * (grad_probs - row_delta[:, None])).astype(jnp.bfloat16)
    grad_query = (
        jnp.einsum("qk,kd->qd", grad_scores, key_rows, preferred_element_type=jnp.float32) * scaling
    )
    grad_key = (
        jnp.einsum("qk,qd->kd", grad_scores, query_rows, preferred_element_type=jnp.float32)
        * scaling
    )
    results = results + (grad_query, grad_key)
    return results


def pick_rows(input_matrix, start_shift):
    if input_matrix.ndim == 1:
        reshaped_tensor = input_matrix.reshape(
            input_matrix.shape[0] // DILATION_STEP, DILATION_STEP
        )
        return lax.dynamic_index_in_dim(reshaped_tensor, start_shift, axis=1, keepdims=False)
    width = input_matrix.shape[1]
    return lax.dynamic_slice_in_dim(dense(input_matrix), start_shift * width, width, 1)


def spread_rows(input_matrix, start_shift, filler):
    picked_index = jnp.arange(DILATION_STEP, dtype=jnp.int32) == start_shift
    return jnp.where(picked_index[None, :], input_matrix[:, None], filler).reshape(-1)


def place_cols(input_matrix, start_shift):
    width = input_matrix.shape[1]
    picked_block = jnp.arange(DILATION_STEP * width, dtype=jnp.int32) // width == start_shift
    return jnp.where(picked_block[None, :], jnp.tile(input_matrix, (1, DILATION_STEP)), 0.0)


def by_segment(input_matrix):
    return input_matrix.reshape((input_matrix.shape[0] // SEG, SEG) + input_matrix.shape[1:])


def head_stats(query, key, value, usable, start_shift, scaling):
    seq_rows = query.shape[0]

    def segment_stats(pieces):
        row_max, totals, summed = block_stats(pieces[0], pieces[1], pieces[2], pieces[3], scaling)
        return (row_max, totals, dense(summed))

    max_w, sum_w, acc_w = lax.map(
        segment_stats, (by_segment(query), by_segment(key), by_segment(value), by_segment(usable))
    )
    usable_d = pick_rows(usable, start_shift)
    max_d, sum_d, acc_d = block_stats(
        pick_rows(query, start_shift),
        pick_rows(key, start_shift),
        pick_rows(value, start_shift),
        usable_d,
        scaling,
    )
    return (
        max_w.reshape(seq_rows),
        sum_w.reshape(seq_rows),
        acc_w.reshape(seq_rows // DILATION_STEP, -1),
        spread_rows(max_d, start_shift, NEG),
        spread_rows(sum_d, start_shift, 0.0),
        place_cols(acc_d, start_shift),
    )


def normalizer(statistics, grad, usable):
    max_w, sum_w, acc_w, max_d, sum_d, acc_d = statistics
    largest = jnp.maximum(max_w, max_d)
    totals = sum_w * jnp.exp(max_w - largest) + sum_d * jnp.exp(max_d - largest)
    log_norm = jnp.where(usable, largest + jnp.log(jnp.where(usable, totals, 1.0)), 0.0)
    weight_window = jnp.repeat(jnp.exp(max_w - log_norm).reshape(-1, DILATION_STEP), HD, axis=1)
    weight_dilated = jnp.repeat(jnp.exp(max_d - log_norm).reshape(-1, DILATION_STEP), HD, axis=1)
    attended = weight_window * acc_w + weight_dilated * acc_d
    products = dense(grad).astype(jnp.float32) * attended
    row_delta = jnp.sum(products.reshape(products.shape[0], DILATION_STEP, HD), axis=2).reshape(-1)
    return (log_norm, row_delta)


def head_grads(query, key, value, grad, usable, start_shift, log_norm, row_delta, scaling):
    seq_rows = query.shape[0]

    def segment_grads(pieces):
        parts_out = block_grads(
            pieces[0], pieces[1], pieces[2], pieces[3], pieces[4], pieces[5], pieces[6], scaling
        )
        return tuple((dense(entry) for entry in parts_out))

    window = lax.map(
        segment_grads,
        (
            by_segment(query),
            by_segment(key),
            by_segment(value),
            by_segment(grad),
            by_segment(usable),
            by_segment(log_norm),
            by_segment(row_delta),
        ),
    )
    dilated = block_grads(
        pick_rows(query, start_shift),
        pick_rows(key, start_shift),
        pick_rows(value, start_shift),
        pick_rows(grad, start_shift),
        pick_rows(usable, start_shift),
        pick_rows(log_norm, start_shift),
        pick_rows(row_delta, start_shift),
        scaling,
    )
    return tuple(
        (
            first.reshape(seq_rows // DILATION_STEP, -1) + place_cols(second, start_shift)
            for first, second in zip(window, dilated)
        )
    )


def columns(input_matrix, local_head):
    return input_matrix[:, local_head * HD : (local_head + 1) * HD]


def join_heads(dense_list, seq_rows):
    pieces = [entry.reshape(seq_rows, HD) for entry in dense_list]
    if len(pieces) == 1:
        return pieces[0].astype(jnp.bfloat16)
    return jnp.concatenate(pieces, axis=1).astype(jnp.bfloat16)


def on_device(queries, keys, values, out_grad, tissue, valid_count):
    tissue_flags = lax.all_gather(tissue, "seq", axis=0, tiled=True)
    head_queries, head_keys, head_values, head_grad = (
        lax.all_to_all(queries, "seq", split_axis=1, concat_axis=0, tiled=True),
        lax.all_to_all(keys, "seq", split_axis=1, concat_axis=0, tiled=True),
        lax.all_to_all(values, "seq", split_axis=1, concat_axis=0, tiled=True),
        lax.all_to_all(out_grad, "seq", split_axis=1, concat_axis=0, tiled=True),
    )
    seq_rows = head_queries.shape[0]
    heads_here = head_queries.shape[1] // HD
    block_rows = seq_rows // tissue_flags.shape[0]
    row_index = jnp.arange(seq_rows, dtype=jnp.int32)
    tissue_rows = jnp.broadcast_to(
        tissue_flags[:, None] == 1, (tissue_flags.shape[0], block_rows)
    ).reshape(seq_rows)
    usable = (row_index < valid_count[0]) & tissue_rows
    scaling = 1.0 / math.sqrt(HD)
    leading_head = lax.axis_index("seq") * heads_here
    start_shifts = [(leading_head + local_head) % DILATION_STEP for local_head in range(heads_here)]
    statistics = [
        head_stats(
            columns(head_queries, local_head),
            columns(head_keys, local_head),
            columns(head_values, local_head),
            usable,
            start_shifts[local_head],
            scaling,
        )
        for local_head in range(heads_here)
    ]
    normalized = [
        normalizer(statistics[local_head], columns(head_grad, local_head), usable)
        for local_head in range(heads_here)
    ]

    def grads_of(local_head):
        return head_grads(
            columns(head_queries, local_head),
            columns(head_keys, local_head),
            columns(head_values, local_head),
            columns(head_grad, local_head),
            usable,
            start_shifts[local_head],
            normalized[local_head][0],
            normalized[local_head][1],
            scaling,
        )

    results = [grads_of(local_head) for local_head in range(heads_here)]
    value_part = join_heads([entry[0] for entry in results], seq_rows)
    query_part = join_heads([entry[1] for entry in results], seq_rows)
    key_part = join_heads([entry[2] for entry in results], seq_rows)
    grad_query, grad_key, grad_value = (
        lax.all_to_all(query_part, "seq", split_axis=0, concat_axis=1, tiled=True),
        lax.all_to_all(key_part, "seq", split_axis=0, concat_axis=1, tiled=True),
        lax.all_to_all(value_part, "seq", split_axis=0, concat_axis=1, tiled=True),
    )
    return (grad_query, grad_key, grad_value)


PAIR = 2 * HD
QB = 256
FLOOR = -1e29
FAR_FIRST = (6, 2, 4, 7, 3, 5, 1)
NEAR_FIRST = (1, 2, 4, 3, 5, 6, 7)


def log2_pieces():
    left, pieces = math.log(2.0), []
    for _ in range(3):
        piece = float(np.asarray(left, jnp.bfloat16))
        pieces.append(piece)
        left -= piece
    return pieces


def partner(me, step):
    other = me
    for bit in (1, 2, 4):
        other = other + bit * (1 - 2 * ((me // bit) % 2)) * ((step // bit) % 2)
    return other


def nt_dot(a, b):
    return lax.dot_general(a, b, (((1,), (1,)), ((), ())), preferred_element_type=jnp.float32)


def fused_kernel(
    n,
    q_ref,
    k_ref,
    v_ref,
    g_ref,
    tissue_ref,
    count_ref,
    grads_ref,
    buf,
    flags,
    key_side,
    query_side,
    key_cols,
    sums,
    res,
    flag_send,
    flag_recv,
    in_send,
    in_recv,
    out_send,
    out_recv,
    local_sem,
    tissue_here,
):
    me = lax.axis_index("seq")
    local = q_ref.shape[0]
    rows = n * local
    pairs = buf.shape[0]
    width = pairs * PAIR
    chip = QB // local
    scaling = 1.0 / math.sqrt(HD)
    peers = [partner(me, step) for step in range(n)]

    def rows_of(device):
        return pl.ds(pl.multiple_of(device * local, local), local)

    def cols_of(device, pair):
        return pl.ds(pl.multiple_of(device * width + pair * PAIR, PAIR), PAIR)

    def remote(src, dst, send, recv, device):
        return pltpu.make_async_remote_copy(
            src_ref=src,
            dst_ref=dst,
            send_sem=send,
            recv_sem=recv,
            device_id={"seq": device},
            device_id_type=pl.DeviceIdType.MESH,
        )

    barrier = pltpu.get_barrier_semaphore()
    for step in range(1, n):
        pl.semaphore_signal(
            barrier, inc=1, device_id={"seq": peers[step]}, device_id_type=pl.DeviceIdType.MESH
        )

    small = [
        pltpu.make_async_copy(tissue_ref, tissue_here, local_sem.at[7 * pairs]),
    ]
    for copy in small:
        copy.start()
    ins = (k_ref, v_ref, q_ref, g_ref)
    own = []
    for pair in range(pairs):
        for which in range(4):
            own.append(
                pltpu.make_async_copy(
                    ins[which].at[:, cols_of(me, pair)],
                    buf.at[pair, which, rows_of(me), :],
                    local_sem.at[pair * 4 + which],
                )
            )
    for copy in own:
        copy.start()
    for copy in small:
        copy.wait()
    spot = lax.broadcasted_iota(jnp.int32, flags.shape[1:], 1)
    blocks_here = tissue_here.shape[0]
    tissue = jnp.zeros_like(spot)
    for block in range(blocks_here):
        tissue = jnp.where(spot // (local // blocks_here) == block, tissue_here[block], tissue)
    usable = (me * local + spot < count_ref[0]) & (tissue == 1)
    flags[me] = usable.astype(jnp.float32)
    pl.semaphore_wait(barrier, n - 1)

    def in_copy(pair, which, step):
        return remote(
            ins[which].at[:, cols_of(partner(me, step), pair)],
            buf.at[pair, which, rows_of(me), :],
            in_send.at[pair, which, step],
            in_recv.at[pair, which, step],
            partner(me, step),
        )

    flag_copies = [
        remote(flags.at[me], flags.at[me], flag_send.at[step], flag_recv.at[step], peers[step])
        for step in FAR_FIRST
    ]
    for copy in flag_copies:
        copy.start()
    for pair in range(pairs):
        for group, order in (((0, 1), FAR_FIRST), ((2, 3), NEAR_FIRST)):
            for step in order:
                for which in group:
                    in_copy(pair, which, step).start()

    for copy in own:
        copy.wait()
    for copy in flag_copies:
        copy.wait_recv()
    lane = lax.broadcasted_iota(jnp.int32, (local, PAIR), 1)
    residue = lax.broadcasted_iota(jnp.int32, (local, PAIR), 0) % DILATION_STEP
    pieces = log2_pieces()
    piece = jnp.where(lane < 8, pieces[0], jnp.where(lane < 16, pieces[1], pieces[2]))
    same = (lane < 24) & (lane % DILATION_STEP == residue)
    for block in range(n):
        flag = jnp.transpose(jnp.broadcast_to(flags[block, 0:1, :], (local, PAIR)))
        off = (1.0 - flag) * NEG
        side = jnp.where(lane == 24, off, jnp.where(lane == 25, 1.0, jnp.where(same, piece, 0.0)))
        here = pl.ds(block * local, local)
        for pair in range(pairs):
            key_side[pair, here, PAIR:] = side.astype(jnp.bfloat16)
        for head in range(2 * pairs):
            shift = (me * 2 * pairs + head) % DILATION_STEP
            chosen = same & (lane % DILATION_STEP == shift)
            side = jnp.where(
                lane == 24, 1.0, jnp.where(lane == 25, off, jnp.where(chosen, 1.0, 0.0))
            )
            query_side[head, here, :] = side.astype(jnp.bfloat16)

    half = lax.broadcasted_iota(jnp.int32, (QB, PAIR), 1) // HD
    own_out = []

    def out_copy(pair, which, step):
        device = partner(me, step)
        return remote(
            res.at[pair, which, rows_of(device), :],
            grads_ref.at[which, :, cols_of(me, pair)],
            out_send.at[pair, which, step],
            out_recv.at[pair, which, step],
            device,
        )

    for pair in range(pairs):
        for which in range(2):
            for step in FAR_FIRST:
                in_copy(pair, which, step).wait_recv()
        key_side[pair, :, :PAIR] = buf[pair, 0]
        key_cols[...] = jnp.transpose(buf[pair, 0].astype(jnp.float32)).astype(jnp.bfloat16)
        sums[...] = jnp.zeros_like(sums)

        def query_block(index, carry, pair=pair):
            far = index if pair == 0 else n // chip - 1 - index
            for part in range(chip):
                step = far * chip + part

                def arrived(step=step):
                    for which in (2, 3):
                        in_copy(pair, which, step).wait_recv()

                if part == 0:
                    pl.when(step > 0)(arrived)
                else:
                    arrived()
            first = partner(me - me % chip, far * chip)
            here = pl.ds(pl.multiple_of(first * local, QB), QB)
            query = buf[pair, 2, here, :].astype(jnp.float32) * scaling
            grad = buf[pair, 3, here, :].astype(jnp.float32)
            columns_out = []
            for side in range(2):
                query_h = jnp.where(half == side, query, 0.0).astype(jnp.bfloat16)
                grad_h = jnp.where(half == side, grad, 0.0).astype(jnp.bfloat16)
                extended = jnp.concatenate(
                    [query_h, query_side[2 * pair + side, here, :]], axis=1
                )
                score = nt_dot(key_side[pair], extended)
                grad_prob = nt_dot(buf[pair, 1], grad_h)
                top = jnp.maximum(jnp.max(score, axis=0, keepdims=True), FLOOR)
                weight = jnp.exp(score - top)
                total = jnp.maximum(jnp.sum(weight, axis=0, keepdims=True), 1.0)
                inverse = 1.0 / total
                delta = jnp.sum(weight * grad_prob, axis=0, keepdims=True) * inverse
                prob = weight * inverse
                dscore = (prob * (grad_prob - delta)).astype(jnp.bfloat16)
                sums[0] += jnp.dot(dscore, query_h, preferred_element_type=jnp.float32)
                sums[1] += jnp.dot(
                    prob.astype(jnp.bfloat16), grad_h, preferred_element_type=jnp.float32
                )
                columns_out.append(
                    jnp.dot(
                        key_cols[side * HD : (side + 1) * HD, :],
                        dscore,
                        preferred_element_type=jnp.float32,
                    )
                )
            grad_query = jnp.transpose(jnp.concatenate(columns_out, axis=0)) * scaling
            res[pair, 0, here, :] = grad_query.astype(jnp.bfloat16)
            for part in range(chip):
                step = far * chip + part

                def leaves(step=step):
                    out_copy(pair, 0, step).start()

                if part == 0:
                    pl.when(step > 0)(leaves)
                else:
                    leaves()
            return carry

        lax.fori_loop(0, rows // QB, query_block, 0)
        res[pair, 1] = sums[0].astype(jnp.bfloat16)
        res[pair, 2] = sums[1].astype(jnp.bfloat16)
        for which in range(1, 3):
            for step in FAR_FIRST:
                out_copy(pair, which, step).start()
        for which in range(3):
            copy = pltpu.make_async_copy(
                res.at[pair, which, rows_of(me), :],
                grads_ref.at[which, :, cols_of(me, pair)],
                local_sem.at[4 * pairs + pair * 3 + which],
            )
            copy.start()
            own_out.append(copy)
    for copy in flag_copies:
        copy.wait_send()
    for copy in own_out:
        copy.wait()
    for pair in range(pairs):
        for step in FAR_FIRST:
            for which in range(4):
                in_copy(pair, which, step).wait_send()
            for which in range(3):
                out_copy(pair, which, step).wait()


def write_kernel(grads_ref, dq_ref, dk_ref, dv_ref, sem):
    copies = [
        pltpu.make_async_copy(grads_ref.at[which], out, sem.at[which])
        for which, out in enumerate((dq_ref, dk_ref, dv_ref))
    ]
    for copy in copies:
        copy.start()
    for copy in copies:
        copy.wait()


def on_device_fused(n, queries, keys, values, out_grad, tissue, valid_count):
    local, features = queries.shape
    rows = n * local
    pairs = features // n // PAIR
    hbm = pl.BlockSpec(memory_space=pltpu.HBM)
    vmem = pl.BlockSpec(memory_space=pltpu.VMEM)
    smem = pl.BlockSpec(memory_space=pltpu.SMEM)
    dma = pltpu.SemaphoreType.DMA
    grads = pl.pallas_call(
        functools.partial(fused_kernel, n),
        out_shape=pltpu.VMEM((3, local, features), jnp.bfloat16),
        in_specs=[hbm] * 5 + [smem],
        out_specs=vmem,
        scratch_shapes=[
            pltpu.VMEM((pairs, 4, rows, PAIR), jnp.bfloat16),
            pltpu.VMEM((n, 8, local), jnp.float32),
            pltpu.VMEM((pairs, rows, 2 * PAIR), jnp.bfloat16),
            pltpu.VMEM((2 * pairs, rows, PAIR), jnp.bfloat16),
            pltpu.VMEM((PAIR, rows), jnp.bfloat16),
            pltpu.VMEM((2, rows, PAIR), jnp.float32),
            pltpu.VMEM((pairs, 3, rows, PAIR), jnp.bfloat16),
            dma((n,)),
            dma((n,)),
            dma((pairs, 4, n)),
            dma((pairs, 4, n)),
            dma((pairs, 3, n)),
            dma((pairs, 3, n)),
            dma((7 * pairs + 1,)),
            pltpu.SMEM(tissue.shape, jnp.int32),
        ],
        compiler_params=pltpu.CompilerParams(
            collective_id=0, has_side_effects=True, vmem_limit_bytes=48 * 2**20
        ),
        name="attention_backward",
    )(
        *(
            pltpu.with_memory_space_constraint(entry, pltpu.HBM)
            for entry in (queries, keys, values, out_grad, tissue)
        ),
        valid_count,
    )
    return tuple(
        pl.pallas_call(
            write_kernel,
            out_shape=[jax.ShapeDtypeStruct((local, features), jnp.bfloat16)] * 3,
            in_specs=[vmem],
            out_specs=[hbm] * 3,
            scratch_shapes=[dma((3,))],
            compiler_params=pltpu.CompilerParams(vmem_limit_bytes=4 * 2**20),
            name="write_gradients",
        )(grads)
    )


def solution(mesh):
    in_specs = (
        P(("slide", "seq"), None),
        P(("slide", "seq"), None),
        P(("slide", "seq"), None),
        P(("slide", "seq"), None),
        P(("slide", "seq")),
        P("slide"),
    )
    out_specs = (P(("slide", "seq"), None), P(("slide", "seq"), None), P(("slide", "seq"), None))
    n = mesh.shape["seq"]

    def body(queries, keys, values, out_grad, tissue, valid_count):
        arguments = (queries, keys, values, out_grad, tissue, valid_count)
        local, features = queries.shape
        if n == 8 and local == PAIR and n * local == SEG and features % (n * PAIR) == 0:
            return on_device_fused(n, *arguments)
        return on_device(*arguments)

    return jax.shard_map(
        body, mesh=mesh, in_specs=in_specs, out_specs=out_specs, check_vma=False
    )
```

```python
import functools
import math

import jax
import jax.numpy as jnp
import numpy as np
from jax import lax
from jax.experimental import pallas as pl
from jax.experimental.pallas import tpu as pltpu
from jax.sharding import PartitionSpec as P

HD = 64
SEG = 1024
DILATION_STEP = 8


NEG = -1e30


def dense(input_matrix):
    return input_matrix.reshape(
        input_matrix.shape[0] // DILATION_STEP, DILATION_STEP * input_matrix.shape[1]
    )


def block_stats(query_rows, key_rows, value_rows, usable, scaling):
    scores = (
        jnp.einsum("qd,kd->qk", query_rows, key_rows, preferred_element_type=jnp.float32) * scaling
    )
    allowed = usable[:, None] & usable[None, :]
    row_max = jnp.max(jnp.where(allowed, scores, NEG), axis=1)
    weights = jnp.where(allowed, jnp.exp(scores - row_max[:, None]), 0.0)
    totals = jnp.sum(weights, axis=1)
    summed = jnp.einsum(
        "qk,kd->qd", weights.astype(jnp.bfloat16), value_rows, preferred_element_type=jnp.float32
    )
    return (row_max, totals, summed)


def block_grads(query_rows, key_rows, value_rows, grad_rows, usable, log_norm, row_delta, scaling):
    scores = (
        jnp.einsum("qd,kd->qk", query_rows, key_rows, preferred_element_type=jnp.float32) * scaling
    )
    allowed = usable[:, None] & usable[None, :]
    probs = jnp.where(allowed, jnp.exp(scores - log_norm[:, None]), 0.0)
    results = ()
    results = results + (
        jnp.einsum(
            "qk,qd->kd", probs.astype(jnp.bfloat16), grad_rows, preferred_element_type=jnp.float32
        ),
    )
    grad_probs = jnp.einsum("qd,kd->qk", grad_rows, value_rows, preferred_element_type=jnp.float32)
    grad_scores = (probs * (grad_probs - row_delta[:, None])).astype(jnp.bfloat16)
    grad_query = (
        jnp.einsum("qk,kd->qd", grad_scores, key_rows, preferred_element_type=jnp.float32) * scaling
    )
    grad_key = (
        jnp.einsum("qk,qd->kd", grad_scores, query_rows, preferred_element_type=jnp.float32)
        * scaling
    )
    results = results + (grad_query, grad_key)
    return results


def pick_rows(input_matrix, start_shift):
    if input_matrix.ndim == 1:
        reshaped_tensor = input_matrix.reshape(
            input_matrix.shape[0] // DILATION_STEP, DILATION_STEP
        )
        return lax.dynamic_index_in_dim(reshaped_tensor, start_shift, axis=1, keepdims=False)
    width = input_matrix.shape[1]
    return lax.dynamic_slice_in_dim(dense(input_matrix), start_shift * width, width, 1)


def spread_rows(input_matrix, start_shift, filler):
    picked_index = jnp.arange(DILATION_STEP, dtype=jnp.int32) == start_shift
    return jnp.where(picked_index[None, :], input_matrix[:, None], filler).reshape(-1)


def place_cols(input_matrix, start_shift):
    width = input_matrix.shape[1]
    picked_block = jnp.arange(DILATION_STEP * width, dtype=jnp.int32) // width == start_shift
    return jnp.where(picked_block[None, :], jnp.tile(input_matrix, (1, DILATION_STEP)), 0.0)


def by_segment(input_matrix):
    return input_matrix.reshape((input_matrix.shape[0] // SEG, SEG) + input_matrix.shape[1:])


def head_stats(query, key, value, usable, start_shift, scaling):
    seq_rows = query.shape[0]

    def segment_stats(pieces):
        row_max, totals, summed = block_stats(pieces[0], pieces[1], pieces[2], pieces[3], scaling)
        return (row_max, totals, dense(summed))

    max_w, sum_w, acc_w = lax.map(
        segment_stats, (by_segment(query), by_segment(key), by_segment(value), by_segment(usable))
    )
    usable_d = pick_rows(usable, start_shift)
    max_d, sum_d, acc_d = block_stats(
        pick_rows(query, start_shift),
        pick_rows(key, start_shift),
        pick_rows(value, start_shift),
        usable_d,
        scaling,
    )
    return (
        max_w.reshape(seq_rows),
        sum_w.reshape(seq_rows),
        acc_w.reshape(seq_rows // DILATION_STEP, -1),
        spread_rows(max_d, start_shift, NEG),
        spread_rows(sum_d, start_shift, 0.0),
        place_cols(acc_d, start_shift),
    )


def normalizer(statistics, grad, usable):
    max_w, sum_w, acc_w, max_d, sum_d, acc_d = statistics
    largest = jnp.maximum(max_w, max_d)
    totals = sum_w * jnp.exp(max_w - largest) + sum_d * jnp.exp(max_d - largest)
    log_norm = jnp.where(usable, largest + jnp.log(jnp.where(usable, totals, 1.0)), 0.0)
    weight_window = jnp.repeat(jnp.exp(max_w - log_norm).reshape(-1, DILATION_STEP), HD, axis=1)
    weight_dilated = jnp.repeat(jnp.exp(max_d - log_norm).reshape(-1, DILATION_STEP), HD, axis=1)
    attended = weight_window * acc_w + weight_dilated * acc_d
    products = dense(grad).astype(jnp.float32) * attended
    row_delta = jnp.sum(products.reshape(products.shape[0], DILATION_STEP, HD), axis=2).reshape(-1)
    return (log_norm, row_delta)


def head_grads(query, key, value, grad, usable, start_shift, log_norm, row_delta, scaling):
    seq_rows = query.shape[0]

    def segment_grads(pieces):
        parts_out = block_grads(
            pieces[0], pieces[1], pieces[2], pieces[3], pieces[4], pieces[5], pieces[6], scaling
        )
        return tuple((dense(entry) for entry in parts_out))

    window = lax.map(
        segment_grads,
        (
            by_segment(query),
            by_segment(key),
            by_segment(value),
            by_segment(grad),
            by_segment(usable),
            by_segment(log_norm),
            by_segment(row_delta),
        ),
    )
    dilated = block_grads(
        pick_rows(query, start_shift),
        pick_rows(key, start_shift),
        pick_rows(value, start_shift),
        pick_rows(grad, start_shift),
        pick_rows(usable, start_shift),
        pick_rows(log_norm, start_shift),
        pick_rows(row_delta, start_shift),
        scaling,
    )
    return tuple(
        (
            first.reshape(seq_rows // DILATION_STEP, -1) + place_cols(second, start_shift)
            for first, second in zip(window, dilated)
        )
    )


def columns(input_matrix, local_head):
    return input_matrix[:, local_head * HD : (local_head + 1) * HD]


def join_heads(dense_list, seq_rows):
    pieces = [entry.reshape(seq_rows, HD) for entry in dense_list]
    if len(pieces) == 1:
        return pieces[0].astype(jnp.bfloat16)
    return jnp.concatenate(pieces, axis=1).astype(jnp.bfloat16)


def on_device(queries, keys, values, out_grad, tissue, valid_count):
    tissue_flags = lax.all_gather(tissue, "seq", axis=0, tiled=True)
    head_queries, head_keys, head_values, head_grad = (
        lax.all_to_all(queries, "seq", split_axis=1, concat_axis=0, tiled=True),
        lax.all_to_all(keys, "seq", split_axis=1, concat_axis=0, tiled=True),
        lax.all_to_all(values, "seq", split_axis=1, concat_axis=0, tiled=True),
        lax.all_to_all(out_grad, "seq", split_axis=1, concat_axis=0, tiled=True),
    )
    seq_rows = head_queries.shape[0]
    heads_here = head_queries.shape[1] // HD
    block_rows = seq_rows // tissue_flags.shape[0]
    row_index = jnp.arange(seq_rows, dtype=jnp.int32)
    tissue_rows = jnp.broadcast_to(
        tissue_flags[:, None] == 1, (tissue_flags.shape[0], block_rows)
    ).reshape(seq_rows)
    usable = (row_index < valid_count[0]) & tissue_rows
    scaling = 1.0 / math.sqrt(HD)
    leading_head = lax.axis_index("seq") * heads_here
    start_shifts = [(leading_head + local_head) % DILATION_STEP for local_head in range(heads_here)]
    statistics = [
        head_stats(
            columns(head_queries, local_head),
            columns(head_keys, local_head),
            columns(head_values, local_head),
            usable,
            start_shifts[local_head],
            scaling,
        )
        for local_head in range(heads_here)
    ]
    normalized = [
        normalizer(statistics[local_head], columns(head_grad, local_head), usable)
        for local_head in range(heads_here)
    ]

    def grads_of(local_head):
        return head_grads(
            columns(head_queries, local_head),
            columns(head_keys, local_head),
            columns(head_values, local_head),
            columns(head_grad, local_head),
            usable,
            start_shifts[local_head],
            normalized[local_head][0],
            normalized[local_head][1],
            scaling,
        )

    results = [grads_of(local_head) for local_head in range(heads_here)]
    value_part = join_heads([entry[0] for entry in results], seq_rows)
    query_part = join_heads([entry[1] for entry in results], seq_rows)
    key_part = join_heads([entry[2] for entry in results], seq_rows)
    grad_query, grad_key, grad_value = (
        lax.all_to_all(query_part, "seq", split_axis=0, concat_axis=1, tiled=True),
        lax.all_to_all(key_part, "seq", split_axis=0, concat_axis=1, tiled=True),
        lax.all_to_all(value_part, "seq", split_axis=0, concat_axis=1, tiled=True),
    )
    return (grad_query, grad_key, grad_value)


PAIR = 2 * HD
QB = 256
FLOOR = -1e29
FAR_FIRST = (6, 2, 4, 7, 3, 5, 1)
ONCE = 8


def log2_pieces():
    left, pieces = math.log(2.0), []
    for _ in range(3):
        piece = float(np.asarray(left, jnp.bfloat16))
        pieces.append(piece)
        left -= piece
    return pieces


def partner(me, step):
    other = me
    for bit in (1, 2, 4):
        other = other + bit * (1 - 2 * ((me // bit) % 2)) * ((step // bit) % 2)
    return other


def nt_dot(a, b):
    return lax.dot_general(a, b, (((1,), (1,)), ((), ())), preferred_element_type=jnp.float32)


def fused_kernel(
    n,
    q_ref,
    k_ref,
    v_ref,
    g_ref,
    tissue_ref,
    count_ref,
    grads_ref,
    buf,
    flags,
    key_side,
    query_side,
    key_cols,
    sums,
    res,
    arrive,
    once,
    tissue_here,
):
    me = lax.axis_index("seq")
    local = q_ref.shape[0]
    rows = n * local
    pairs = buf.shape[0]
    width = pairs * PAIR
    chip = QB // local
    scaling = 1.0 / math.sqrt(HD)
    peers = [partner(me, step) for step in range(n)]

    def rows_of(device):
        return pl.ds(pl.multiple_of(device * local, local), local)

    def cols_of(device, pair):
        return pl.ds(pl.multiple_of(device * width + pair * PAIR, PAIR), PAIR)

    def remote(src, dst, send, recv, device):
        return pltpu.make_async_remote_copy(
            src_ref=src,
            dst_ref=dst,
            send_sem=send,
            recv_sem=recv,
            device_id={"seq": device},
            device_id_type=pl.DeviceIdType.MESH,
        )

    barrier = pltpu.get_barrier_semaphore()
    for step in range(1, n):
        pl.semaphore_signal(
            barrier, inc=1, device_id={"seq": peers[step]}, device_id_type=pl.DeviceIdType.MESH
        )

    flag_send, flag_recv, in_send, out_send, out_recv, own_in, own_out, small = (
        once.at[index] for index in range(ONCE)
    )
    tissue_copy = pltpu.make_async_copy(tissue_ref, tissue_here, small)
    tissue_copy.start()
    ins = (k_ref, v_ref, q_ref, g_ref)
    for pair in range(pairs):
        for which in range(4):
            pltpu.make_async_copy(
                ins[which].at[:, cols_of(me, pair)], buf.at[pair, which, rows_of(me), :], own_in
            ).start()
    tissue_copy.wait()
    spot = lax.broadcasted_iota(jnp.int32, flags.shape[1:], 1)
    blocks_here = tissue_here.shape[0]
    tissue = jnp.zeros_like(spot)
    for block in range(blocks_here):
        tissue = jnp.where(spot // (local // blocks_here) == block, tissue_here[block], tissue)
    usable = (me * local + spot < count_ref[0]) & (tissue == 1)
    flags[me] = usable.astype(jnp.float32)
    pl.semaphore_wait(barrier, n - 1)

    for step in FAR_FIRST:
        remote(flags.at[me], flags.at[me], flag_send, flag_recv, peers[step]).start()
    for pair in range(pairs):
        for group in ((0, 1), (2, 3)):
            for step in FAR_FIRST:
                for which in group:
                    spot = 0 if group[0] == 0 else 1 + step // chip
                    remote(
                        ins[which].at[:, cols_of(peers[step], pair)],
                        buf.at[pair, which, rows_of(me), :],
                        in_send,
                        arrive.at[pair, spot],
                        peers[step],
                    ).start()

    def landed(ref, sem):
        remote(ref, ref, in_send, sem, peers[1]).wait_recv()

    def left(ref, sem):
        remote(ref, ref, sem, out_recv, peers[1]).wait_send()

    theirs = pl.ds(0, rows - local)
    mine = buf.at[:, :, pl.ds(0, local), :]
    pltpu.make_async_copy(mine, mine, own_in).wait()
    landed(flags.at[pl.ds(0, n - 1)], flag_recv)
    lane = lax.broadcasted_iota(jnp.int32, (local, PAIR), 1)
    residue = lax.broadcasted_iota(jnp.int32, (local, PAIR), 0) % DILATION_STEP
    pieces = log2_pieces()
    piece = jnp.where(lane < 8, pieces[0], jnp.where(lane < 16, pieces[1], pieces[2]))
    same = (lane < 24) & (lane % DILATION_STEP == residue)
    for block in range(n):
        flag = jnp.transpose(jnp.broadcast_to(flags[block, 0:1, :], (local, PAIR)))
        off = (1.0 - flag) * NEG
        side = jnp.where(lane == 24, off, jnp.where(lane == 25, 1.0, jnp.where(same, piece, 0.0)))
        here = pl.ds(block * local, local)
        for pair in range(pairs):
            key_side[pair, here, PAIR:] = side.astype(jnp.bfloat16)
        for head in range(2 * pairs):
            shift = (me * 2 * pairs + head) % DILATION_STEP
            chosen = same & (lane % DILATION_STEP == shift)
            side = jnp.where(
                lane == 24, 1.0, jnp.where(lane == 25, off, jnp.where(chosen, 1.0, 0.0))
            )
            query_side[head, here, :] = side.astype(jnp.bfloat16)

    half = lax.broadcasted_iota(jnp.int32, (QB, PAIR), 1) // HD

    def send_out(pair, which, device):
        remote(
            res.at[pair, which, rows_of(device), :],
            grads_ref.at[which, :, cols_of(me, pair)],
            out_send,
            out_recv,
            device,
        ).start()

    for pair in range(pairs):
        landed(buf.at[pair, pl.ds(0, 2), theirs, :], arrive.at[pair, 0])
        key_side[pair, :, :PAIR] = buf[pair, 0]
        key_cols[...] = jnp.transpose(buf[pair, 0].astype(jnp.float32)).astype(jnp.bfloat16)
        sums[...] = jnp.zeros_like(sums)

        def query_block(index, carry, pair=pair):
            far = index if pair == 0 else n // chip - 1 - index
            for count, here in ((chip - 1, far == 0), (chip, far > 0)):

                @pl.when(here)
                def _(count=count):
                    these = pl.ds(0, count * local)
                    landed(buf.at[pair, pl.ds(2, 2), these, :], arrive.at[pair, 1 + far])

            first = partner(me - me % chip, far * chip)
            here = pl.ds(pl.multiple_of(first * local, QB), QB)
            query = buf[pair, 2, here, :].astype(jnp.float32) * scaling
            grad = buf[pair, 3, here, :].astype(jnp.float32)
            columns_out = []
            for side in range(2):
                query_h = jnp.where(half == side, query, 0.0).astype(jnp.bfloat16)
                grad_h = jnp.where(half == side, grad, 0.0).astype(jnp.bfloat16)
                extended = jnp.concatenate(
                    [query_h, query_side[2 * pair + side, here, :]], axis=1
                )
                score = nt_dot(key_side[pair], extended)
                grad_prob = nt_dot(buf[pair, 1], grad_h)
                top = jnp.maximum(jnp.max(score, axis=0, keepdims=True), FLOOR)
                weight = jnp.exp(score - top)
                total = jnp.maximum(jnp.sum(weight, axis=0, keepdims=True), 1.0)
                inverse = 1.0 / total
                delta = jnp.sum(weight * grad_prob, axis=0, keepdims=True) * inverse
                prob = weight * inverse
                dscore = (prob * (grad_prob - delta)).astype(jnp.bfloat16)
                sums[0] += jnp.dot(dscore, query_h, preferred_element_type=jnp.float32)
                sums[1] += jnp.dot(
                    prob.astype(jnp.bfloat16), grad_h, preferred_element_type=jnp.float32
                )
                columns_out.append(
                    jnp.dot(
                        key_cols[side * HD : (side + 1) * HD, :],
                        dscore,
                        preferred_element_type=jnp.float32,
                    )
                )
            grad_query = jnp.transpose(jnp.concatenate(columns_out, axis=0)) * scaling
            res[pair, 0, here, :] = grad_query.astype(jnp.bfloat16)
            for part in range(chip):
                step = far * chip + part

                def leaves(step=step):
                    send_out(pair, 0, partner(me, step))

                if part == 0:
                    pl.when(step > 0)(leaves)
                else:
                    leaves()
            return carry

        lax.fori_loop(0, rows // QB, query_block, 0)
        res[pair, 1] = sums[0].astype(jnp.bfloat16)
        res[pair, 2] = sums[1].astype(jnp.bfloat16)
        for step in FAR_FIRST:
            send_out(pair, pl.ds(1, 2), peers[step])
        pltpu.make_async_copy(
            res.at[pair, :, rows_of(me), :], grads_ref.at[:, :, cols_of(me, pair)], own_out
        ).start()
    left(flags.at[pl.ds(0, n - 1)], flag_send)
    left(buf.at[:, :, theirs, :], in_send)
    mine = res.at[:, :, pl.ds(0, local), :]
    pltpu.make_async_copy(mine, mine, own_out).wait()
    left(res.at[:, :, theirs, :], out_send)
    landed(res.at[:, :, theirs, :], out_recv)


def write_kernel(grads_ref, dq_ref, dk_ref, dv_ref, sem):
    copies = [
        pltpu.make_async_copy(grads_ref.at[which], out, sem.at[which])
        for which, out in enumerate((dq_ref, dk_ref, dv_ref))
    ]
    for copy in copies:
        copy.start()
    for copy in copies:
        copy.wait()


def on_device_fused(n, queries, keys, values, out_grad, tissue, valid_count):
    local, features = queries.shape
    rows = n * local
    pairs = features // n // PAIR
    hbm = pl.BlockSpec(memory_space=pltpu.HBM)
    vmem = pl.BlockSpec(memory_space=pltpu.VMEM)
    smem = pl.BlockSpec(memory_space=pltpu.SMEM)
    dma = pltpu.SemaphoreType.DMA
    grads = pl.pallas_call(
        functools.partial(fused_kernel, n),
        out_shape=pltpu.VMEM((3, local, features), jnp.bfloat16),
        in_specs=[hbm] * 5 + [smem],
        out_specs=vmem,
        scratch_shapes=[
            pltpu.VMEM((pairs, 4, rows, PAIR), jnp.bfloat16),
            pltpu.VMEM((n, 8, local), jnp.float32),
            pltpu.VMEM((pairs, rows, 2 * PAIR), jnp.bfloat16),
            pltpu.VMEM((2 * pairs, rows, PAIR), jnp.bfloat16),
            pltpu.VMEM((PAIR, rows), jnp.bfloat16),
            pltpu.VMEM((2, rows, PAIR), jnp.float32),
            pltpu.VMEM((pairs, 3, rows, PAIR), jnp.bfloat16),
            dma((pairs, 1 + rows // QB)),
            dma((ONCE,)),
            pltpu.SMEM(tissue.shape, jnp.int32),
        ],
        compiler_params=pltpu.CompilerParams(
            collective_id=0, has_side_effects=True, vmem_limit_bytes=48 * 2**20
        ),
        name="attention_backward",
    )(
        *(
            pltpu.with_memory_space_constraint(entry, pltpu.HBM)
            for entry in (queries, keys, values, out_grad, tissue)
        ),
        valid_count,
    )
    return tuple(
        pl.pallas_call(
            write_kernel,
            out_shape=[jax.ShapeDtypeStruct((local, features), jnp.bfloat16)] * 3,
            in_specs=[vmem],
            out_specs=[hbm] * 3,
            scratch_shapes=[dma((3,))],
            compiler_params=pltpu.CompilerParams(vmem_limit_bytes=4 * 2**20),
            name="write_gradients",
        )(grads)
    )


def solution(mesh):
    in_specs = (
        P(("slide", "seq"), None),
        P(("slide", "seq"), None),
        P(("slide", "seq"), None),
        P(("slide", "seq"), None),
        P(("slide", "seq")),
        P("slide"),
    )
    out_specs = (P(("slide", "seq"), None), P(("slide", "seq"), None), P(("slide", "seq"), None))
    n = mesh.shape["seq"]

    def body(queries, keys, values, out_grad, tissue, valid_count):
        arguments = (queries, keys, values, out_grad, tissue, valid_count)
        local, features = queries.shape
        if n == 8 and local == PAIR and n * local == SEG and features % (n * PAIR) == 0:
            return on_device_fused(n, *arguments)
        return on_device(*arguments)

    return jax.shard_map(
        body, mesh=mesh, in_specs=in_specs, out_specs=out_specs, check_vma=False
    )
```

```python
import functools
import math

import jax
import jax.numpy as jnp
import numpy as np
from jax import lax
from jax.experimental import pallas as pl
from jax.experimental.pallas import tpu as pltpu
from jax.sharding import PartitionSpec as P

HD = 64
SEG = 1024
DILATION_STEP = 8


NEG = -1e30


def dense(input_matrix):
    return input_matrix.reshape(
        input_matrix.shape[0] // DILATION_STEP, DILATION_STEP * input_matrix.shape[1]
    )


def block_stats(query_rows, key_rows, value_rows, usable, scaling):
    scores = (
        jnp.einsum("qd,kd->qk", query_rows, key_rows, preferred_element_type=jnp.float32) * scaling
    )
    allowed = usable[:, None] & usable[None, :]
    row_max = jnp.max(jnp.where(allowed, scores, NEG), axis=1)
    weights = jnp.where(allowed, jnp.exp(scores - row_max[:, None]), 0.0)
    totals = jnp.sum(weights, axis=1)
    summed = jnp.einsum(
        "qk,kd->qd", weights.astype(jnp.bfloat16), value_rows, preferred_element_type=jnp.float32
    )
    return (row_max, totals, summed)


def block_grads(query_rows, key_rows, value_rows, grad_rows, usable, log_norm, row_delta, scaling):
    scores = (
        jnp.einsum("qd,kd->qk", query_rows, key_rows, preferred_element_type=jnp.float32) * scaling
    )
    allowed = usable[:, None] & usable[None, :]
    probs = jnp.where(allowed, jnp.exp(scores - log_norm[:, None]), 0.0)
    results = ()
    results = results + (
        jnp.einsum(
            "qk,qd->kd", probs.astype(jnp.bfloat16), grad_rows, preferred_element_type=jnp.float32
        ),
    )
    grad_probs = jnp.einsum("qd,kd->qk", grad_rows, value_rows, preferred_element_type=jnp.float32)
    grad_scores = (probs * (grad_probs - row_delta[:, None])).astype(jnp.bfloat16)
    grad_query = (
        jnp.einsum("qk,kd->qd", grad_scores, key_rows, preferred_element_type=jnp.float32) * scaling
    )
    grad_key = (
        jnp.einsum("qk,qd->kd", grad_scores, query_rows, preferred_element_type=jnp.float32)
        * scaling
    )
    results = results + (grad_query, grad_key)
    return results


def pick_rows(input_matrix, start_shift):
    if input_matrix.ndim == 1:
        reshaped_tensor = input_matrix.reshape(
            input_matrix.shape[0] // DILATION_STEP, DILATION_STEP
        )
        return lax.dynamic_index_in_dim(reshaped_tensor, start_shift, axis=1, keepdims=False)
    width = input_matrix.shape[1]
    return lax.dynamic_slice_in_dim(dense(input_matrix), start_shift * width, width, 1)


def spread_rows(input_matrix, start_shift, filler):
    picked_index = jnp.arange(DILATION_STEP, dtype=jnp.int32) == start_shift
    return jnp.where(picked_index[None, :], input_matrix[:, None], filler).reshape(-1)


def place_cols(input_matrix, start_shift):
    width = input_matrix.shape[1]
    picked_block = jnp.arange(DILATION_STEP * width, dtype=jnp.int32) // width == start_shift
    return jnp.where(picked_block[None, :], jnp.tile(input_matrix, (1, DILATION_STEP)), 0.0)


def by_segment(input_matrix):
    return input_matrix.reshape((input_matrix.shape[0] // SEG, SEG) + input_matrix.shape[1:])


def head_stats(query, key, value, usable, start_shift, scaling):
    seq_rows = query.shape[0]

    def segment_stats(pieces):
        row_max, totals, summed = block_stats(pieces[0], pieces[1], pieces[2], pieces[3], scaling)
        return (row_max, totals, dense(summed))

    max_w, sum_w, acc_w = lax.map(
        segment_stats, (by_segment(query), by_segment(key), by_segment(value), by_segment(usable))
    )
    usable_d = pick_rows(usable, start_shift)
    max_d, sum_d, acc_d = block_stats(
        pick_rows(query, start_shift),
        pick_rows(key, start_shift),
        pick_rows(value, start_shift),
        usable_d,
        scaling,
    )
    return (
        max_w.reshape(seq_rows),
        sum_w.reshape(seq_rows),
        acc_w.reshape(seq_rows // DILATION_STEP, -1),
        spread_rows(max_d, start_shift, NEG),
        spread_rows(sum_d, start_shift, 0.0),
        place_cols(acc_d, start_shift),
    )


def normalizer(statistics, grad, usable):
    max_w, sum_w, acc_w, max_d, sum_d, acc_d = statistics
    largest = jnp.maximum(max_w, max_d)
    totals = sum_w * jnp.exp(max_w - largest) + sum_d * jnp.exp(max_d - largest)
    log_norm = jnp.where(usable, largest + jnp.log(jnp.where(usable, totals, 1.0)), 0.0)
    weight_window = jnp.repeat(jnp.exp(max_w - log_norm).reshape(-1, DILATION_STEP), HD, axis=1)
    weight_dilated = jnp.repeat(jnp.exp(max_d - log_norm).reshape(-1, DILATION_STEP), HD, axis=1)
    attended = weight_window * acc_w + weight_dilated * acc_d
    products = dense(grad).astype(jnp.float32) * attended
    row_delta = jnp.sum(products.reshape(products.shape[0], DILATION_STEP, HD), axis=2).reshape(-1)
    return (log_norm, row_delta)


def head_grads(query, key, value, grad, usable, start_shift, log_norm, row_delta, scaling):
    seq_rows = query.shape[0]

    def segment_grads(pieces):
        parts_out = block_grads(
            pieces[0], pieces[1], pieces[2], pieces[3], pieces[4], pieces[5], pieces[6], scaling
        )
        return tuple((dense(entry) for entry in parts_out))

    window = lax.map(
        segment_grads,
        (
            by_segment(query),
            by_segment(key),
            by_segment(value),
            by_segment(grad),
            by_segment(usable),
            by_segment(log_norm),
            by_segment(row_delta),
        ),
    )
    dilated = block_grads(
        pick_rows(query, start_shift),
        pick_rows(key, start_shift),
        pick_rows(value, start_shift),
        pick_rows(grad, start_shift),
        pick_rows(usable, start_shift),
        pick_rows(log_norm, start_shift),
        pick_rows(row_delta, start_shift),
        scaling,
    )
    return tuple(
        (
            first.reshape(seq_rows // DILATION_STEP, -1) + place_cols(second, start_shift)
            for first, second in zip(window, dilated)
        )
    )


def columns(input_matrix, local_head):
    return input_matrix[:, local_head * HD : (local_head + 1) * HD]


def join_heads(dense_list, seq_rows):
    pieces = [entry.reshape(seq_rows, HD) for entry in dense_list]
    if len(pieces) == 1:
        return pieces[0].astype(jnp.bfloat16)
    return jnp.concatenate(pieces, axis=1).astype(jnp.bfloat16)


def on_device(queries, keys, values, out_grad, tissue, valid_count):
    tissue_flags = lax.all_gather(tissue, "seq", axis=0, tiled=True)
    head_queries, head_keys, head_values, head_grad = (
        lax.all_to_all(queries, "seq", split_axis=1, concat_axis=0, tiled=True),
        lax.all_to_all(keys, "seq", split_axis=1, concat_axis=0, tiled=True),
        lax.all_to_all(values, "seq", split_axis=1, concat_axis=0, tiled=True),
        lax.all_to_all(out_grad, "seq", split_axis=1, concat_axis=0, tiled=True),
    )
    seq_rows = head_queries.shape[0]
    heads_here = head_queries.shape[1] // HD
    block_rows = seq_rows // tissue_flags.shape[0]
    row_index = jnp.arange(seq_rows, dtype=jnp.int32)
    tissue_rows = jnp.broadcast_to(
        tissue_flags[:, None] == 1, (tissue_flags.shape[0], block_rows)
    ).reshape(seq_rows)
    usable = (row_index < valid_count[0]) & tissue_rows
    scaling = 1.0 / math.sqrt(HD)
    leading_head = lax.axis_index("seq") * heads_here
    start_shifts = [(leading_head + local_head) % DILATION_STEP for local_head in range(heads_here)]
    statistics = [
        head_stats(
            columns(head_queries, local_head),
            columns(head_keys, local_head),
            columns(head_values, local_head),
            usable,
            start_shifts[local_head],
            scaling,
        )
        for local_head in range(heads_here)
    ]
    normalized = [
        normalizer(statistics[local_head], columns(head_grad, local_head), usable)
        for local_head in range(heads_here)
    ]

    def grads_of(local_head):
        return head_grads(
            columns(head_queries, local_head),
            columns(head_keys, local_head),
            columns(head_values, local_head),
            columns(head_grad, local_head),
            usable,
            start_shifts[local_head],
            normalized[local_head][0],
            normalized[local_head][1],
            scaling,
        )

    results = [grads_of(local_head) for local_head in range(heads_here)]
    value_part = join_heads([entry[0] for entry in results], seq_rows)
    query_part = join_heads([entry[1] for entry in results], seq_rows)
    key_part = join_heads([entry[2] for entry in results], seq_rows)
    grad_query, grad_key, grad_value = (
        lax.all_to_all(query_part, "seq", split_axis=0, concat_axis=1, tiled=True),
        lax.all_to_all(key_part, "seq", split_axis=0, concat_axis=1, tiled=True),
        lax.all_to_all(value_part, "seq", split_axis=0, concat_axis=1, tiled=True),
    )
    return (grad_query, grad_key, grad_value)


PAIR = 2 * HD
QB = 256
FLOOR = -1e29
PEER_ORDER = (1, 6, 7, 2, 3, 4, 5)
ONCE = 8


def log2_pieces():
    left, pieces = math.log(2.0), []
    for _ in range(3):
        piece = float(np.asarray(left, jnp.bfloat16))
        pieces.append(piece)
        left -= piece
    return pieces


def partner(me, step):
    other = me
    for bit in (1, 2, 4):
        other = other + bit * (1 - 2 * ((me // bit) % 2)) * ((step // bit) % 2)
    return other


def nt_dot(a, b):
    return lax.dot_general(a, b, (((1,), (1,)), ((), ())), preferred_element_type=jnp.float32)


def fused_kernel(
    n,
    q_ref,
    k_ref,
    v_ref,
    g_ref,
    tissue_ref,
    count_ref,
    grads_ref,
    buf,
    flags,
    key_side,
    query_side,
    key_cols,
    sums,
    res,
    arrive,
    once,
    tissue_here,
):
    me = lax.axis_index("seq")
    local = q_ref.shape[0]
    rows = n * local
    pairs = buf.shape[0]
    width = pairs * PAIR
    chip = QB // local
    scaling = 1.0 / math.sqrt(HD)
    peers = [partner(me, step) for step in range(n)]

    def rows_of(device):
        return pl.ds(pl.multiple_of(device * local, local), local)

    def cols_of(device, pair):
        return pl.ds(pl.multiple_of(device * width + pair * PAIR, PAIR), PAIR)

    def remote(src, dst, send, recv, device):
        return pltpu.make_async_remote_copy(
            src_ref=src,
            dst_ref=dst,
            send_sem=send,
            recv_sem=recv,
            device_id={"seq": device},
            device_id_type=pl.DeviceIdType.MESH,
        )

    barrier = pltpu.get_barrier_semaphore()
    for step in range(1, n):
        pl.semaphore_signal(
            barrier, inc=1, device_id={"seq": peers[step]}, device_id_type=pl.DeviceIdType.MESH
        )

    flag_send, flag_recv, in_send, out_send, out_recv, own_in, own_out, small = (
        once.at[index] for index in range(ONCE)
    )
    pl.semaphore_wait(barrier, n - 1)

    ins = (k_ref, v_ref, q_ref, g_ref)

    def send_in(pair, group):
        for step in PEER_ORDER:
            for which in range(2 * group, 2 * group + 2):
                remote(
                    ins[which].at[:, cols_of(peers[step], pair)],
                    buf.at[pair, which, rows_of(me), :],
                    in_send,
                    arrive.at[pair, 1 + step // chip if group else 0],
                    peers[step],
                ).start()

    send_in(0, 0)
    tissue_copy = pltpu.make_async_copy(tissue_ref, tissue_here, small)
    tissue_copy.start()
    for pair in range(pairs):
        for which in range(4):
            pltpu.make_async_copy(
                ins[which].at[:, cols_of(me, pair)], buf.at[pair, which, rows_of(me), :], own_in
            ).start()
    tissue_copy.wait()
    spot = lax.broadcasted_iota(jnp.int32, flags.shape[1:], 1)
    blocks_here = tissue_here.shape[0]
    tissue = jnp.zeros_like(spot)
    for block in range(blocks_here):
        tissue = jnp.where(spot // (local // blocks_here) == block, tissue_here[block], tissue)
    usable = (me * local + spot < count_ref[0]) & (tissue == 1)
    flags[me] = usable.astype(jnp.float32)
    for step in PEER_ORDER:
        remote(
            flags.at[me, pl.ds(0, 1)], flags.at[me, pl.ds(0, 1)], flag_send, flag_recv, peers[step]
        ).start()
    send_in(0, 1)
    for pair in range(1, pairs):
        send_in(pair, 0)
        send_in(pair, 1)

    def landed(ref, sem):
        remote(ref, ref, in_send, sem, peers[1]).wait_recv()

    def left(ref, sem):
        remote(ref, ref, sem, out_recv, peers[1]).wait_send()

    theirs = pl.ds(0, rows - local)
    mine = buf.at[:, :, pl.ds(0, local), :]
    pltpu.make_async_copy(mine, mine, own_in).wait()
    landed(flags.at[0, pl.ds(0, n - 1)], flag_recv)
    lane = lax.broadcasted_iota(jnp.int32, (local, PAIR), 1)
    residue = lax.broadcasted_iota(jnp.int32, (local, PAIR), 0) % DILATION_STEP
    pieces = log2_pieces()
    piece = jnp.where(lane < 8, pieces[0], jnp.where(lane < 16, pieces[1], pieces[2]))
    same = (lane < 24) & (lane % DILATION_STEP == residue)
    for block in range(n):
        flag = jnp.transpose(jnp.broadcast_to(flags[block, 0:1, :], (local, PAIR)))
        off = (1.0 - flag) * NEG
        side = jnp.where(lane == 24, off, jnp.where(lane == 25, 1.0, jnp.where(same, piece, 0.0)))
        here = pl.ds(block * local, local)
        for pair in range(pairs):
            key_side[pair, here, PAIR:] = side.astype(jnp.bfloat16)
        for head in range(2 * pairs):
            shift = (me * 2 * pairs + head) % DILATION_STEP
            chosen = same & (lane % DILATION_STEP == shift)
            side = jnp.where(
                lane == 24, 1.0, jnp.where(lane == 25, off, jnp.where(chosen, 1.0, 0.0))
            )
            query_side[head, here, :] = side.astype(jnp.bfloat16)

    half = lax.broadcasted_iota(jnp.int32, (QB, PAIR), 1) // HD

    def send_out(pair, which, device):
        remote(
            res.at[pair, which, rows_of(device), :],
            grads_ref.at[which, :, cols_of(me, pair)],
            out_send,
            out_recv,
            device,
        ).start()

    for pair in range(pairs):
        landed(buf.at[pair, pl.ds(0, 2), theirs, :], arrive.at[pair, 0])
        key_side[pair, :, :PAIR] = buf[pair, 0]
        key_cols[...] = jnp.transpose(buf[pair, 0].astype(jnp.float32)).astype(jnp.bfloat16)
        sums[...] = jnp.zeros_like(sums)

        def query_block(index, carry, pair=pair):
            far = (n // chip - index) % (n // chip) if pair == 0 else n // chip - 1 - index
            for count, here in ((chip - 1, far == 0), (chip, far > 0)):

                @pl.when(here)
                def _(count=count):
                    these = pl.ds(0, count * local)
                    landed(buf.at[pair, pl.ds(2, 2), these, :], arrive.at[pair, 1 + far])

            first = partner(me - me % chip, far * chip)
            here = pl.ds(pl.multiple_of(first * local, QB), QB)
            query = buf[pair, 2, here, :].astype(jnp.float32) * scaling
            grad = buf[pair, 3, here, :].astype(jnp.float32)
            columns_out = []
            for side in range(2):
                query_h = jnp.where(half == side, query, 0.0).astype(jnp.bfloat16)
                grad_h = jnp.where(half == side, grad, 0.0).astype(jnp.bfloat16)
                extended = jnp.concatenate(
                    [query_h, query_side[2 * pair + side, here, :]], axis=1
                )
                score = nt_dot(key_side[pair], extended)
                grad_prob = nt_dot(buf[pair, 1], grad_h)
                top = jnp.maximum(jnp.max(score, axis=0, keepdims=True), FLOOR)
                weight = jnp.exp(score - top)
                total = jnp.maximum(jnp.sum(weight, axis=0, keepdims=True), 1.0)
                inverse = 1.0 / total
                delta = jnp.sum(weight * grad_prob, axis=0, keepdims=True) * inverse
                prob = weight * inverse
                dscore = (prob * (grad_prob - delta)).astype(jnp.bfloat16)
                sums[0] += jnp.dot(dscore, query_h, preferred_element_type=jnp.float32)
                sums[1] += jnp.dot(
                    prob.astype(jnp.bfloat16), grad_h, preferred_element_type=jnp.float32
                )
                columns_out.append(
                    jnp.dot(
                        key_cols[side * HD : (side + 1) * HD, :],
                        dscore,
                        preferred_element_type=jnp.float32,
                    )
                )
            grad_query = jnp.transpose(jnp.concatenate(columns_out, axis=0)) * scaling
            res[pair, 0, here, :] = grad_query.astype(jnp.bfloat16)
            for part in range(chip):
                step = far * chip + part

                def leaves(step=step):
                    send_out(pair, 0, partner(me, step))

                if part == 0:
                    pl.when(step > 0)(leaves)
                else:
                    leaves()
            return carry

        lax.fori_loop(0, rows // QB, query_block, 0)
        res[pair, 1] = sums[0].astype(jnp.bfloat16)
        res[pair, 2] = sums[1].astype(jnp.bfloat16)
        for step in PEER_ORDER:
            send_out(pair, pl.ds(1, 2), peers[step])
        pltpu.make_async_copy(
            res.at[pair, :, rows_of(me), :], grads_ref.at[:, :, cols_of(me, pair)], own_out
        ).start()
    left(flags.at[0, pl.ds(0, n - 1)], flag_send)
    left(buf.at[:, :, theirs, :], in_send)
    mine = res.at[:, :, pl.ds(0, local), :]
    pltpu.make_async_copy(mine, mine, own_out).wait()
    left(res.at[:, :, theirs, :], out_send)
    landed(res.at[:, :, theirs, :], out_recv)


def write_kernel(grads_ref, dq_ref, dk_ref, dv_ref, sem):
    copies = [
        pltpu.make_async_copy(grads_ref.at[which], out, sem.at[0])
        for which, out in enumerate((dq_ref, dk_ref, dv_ref))
    ]
    for copy in copies:
        copy.start()
    for copy in copies:
        copy.wait()


def on_device_fused(n, queries, keys, values, out_grad, tissue, valid_count):
    local, features = queries.shape
    rows = n * local
    pairs = features // n // PAIR
    hbm = pl.BlockSpec(memory_space=pltpu.HBM)
    vmem = pl.BlockSpec(memory_space=pltpu.VMEM)
    smem = pl.BlockSpec(memory_space=pltpu.SMEM)
    dma = pltpu.SemaphoreType.DMA
    grads = pl.pallas_call(
        functools.partial(fused_kernel, n),
        out_shape=pltpu.VMEM((3, local, features), jnp.bfloat16),
        in_specs=[hbm] * 5 + [smem],
        out_specs=vmem,
        scratch_shapes=[
            pltpu.VMEM((pairs, 4, rows, PAIR), jnp.bfloat16),
            pltpu.VMEM((n, 8, local), jnp.float32),
            pltpu.VMEM((pairs, rows, 2 * PAIR), jnp.bfloat16),
            pltpu.VMEM((2 * pairs, rows, PAIR), jnp.bfloat16),
            pltpu.VMEM((PAIR, rows), jnp.bfloat16),
            pltpu.VMEM((2, rows, PAIR), jnp.float32),
            pltpu.VMEM((pairs, 3, rows, PAIR), jnp.bfloat16),
            dma((pairs, 1 + rows // QB)),
            dma((ONCE,)),
            pltpu.SMEM(tissue.shape, jnp.int32),
        ],
        compiler_params=pltpu.CompilerParams(
            collective_id=0, has_side_effects=True, vmem_limit_bytes=48 * 2**20
        ),
        name="attention_backward",
    )(
        *(
            pltpu.with_memory_space_constraint(entry, pltpu.HBM)
            for entry in (queries, keys, values, out_grad, tissue)
        ),
        valid_count,
    )
    return tuple(
        pl.pallas_call(
            write_kernel,
            out_shape=[jax.ShapeDtypeStruct((local, features), jnp.bfloat16)] * 3,
            in_specs=[vmem],
            out_specs=[hbm] * 3,
            scratch_shapes=[dma((1,))],
            compiler_params=pltpu.CompilerParams(vmem_limit_bytes=4 * 2**20),
            name="write_gradients",
        )(grads)
    )


def solution(mesh):
    in_specs = (
        P(("slide", "seq"), None),
        P(("slide", "seq"), None),
        P(("slide", "seq"), None),
        P(("slide", "seq"), None),
        P(("slide", "seq")),
        P("slide"),
    )
    out_specs = (P(("slide", "seq"), None), P(("slide", "seq"), None), P(("slide", "seq"), None))
    n = mesh.shape["seq"]

    def body(queries, keys, values, out_grad, tissue, valid_count):
        arguments = (queries, keys, values, out_grad, tissue, valid_count)
        local, features = queries.shape
        if n == 8 and local == PAIR and n * local == SEG and features % (n * PAIR) == 0:
            return on_device_fused(n, *arguments)
        return on_device(*arguments)

    return jax.shard_map(
        body, mesh=mesh, in_specs=in_specs, out_specs=out_specs, check_vma=False
    )
```

```python
import functools
import math

import jax
import jax.numpy as jnp
import numpy as np
from jax import lax
from jax.experimental import pallas as pl
from jax.experimental.pallas import tpu as pltpu
from jax.sharding import PartitionSpec as P

HD = 64
SEG = 1024
DILATION_STEP = 8


NEG = -1e30


def dense(input_matrix):
    return input_matrix.reshape(
        input_matrix.shape[0] // DILATION_STEP, DILATION_STEP * input_matrix.shape[1]
    )


def block_stats(query_rows, key_rows, value_rows, usable, scaling):
    scores = (
        jnp.einsum("qd,kd->qk", query_rows, key_rows, preferred_element_type=jnp.float32) * scaling
    )
    allowed = usable[:, None] & usable[None, :]
    row_max = jnp.max(jnp.where(allowed, scores, NEG), axis=1)
    weights = jnp.where(allowed, jnp.exp(scores - row_max[:, None]), 0.0)
    totals = jnp.sum(weights, axis=1)
    summed = jnp.einsum(
        "qk,kd->qd", weights.astype(jnp.bfloat16), value_rows, preferred_element_type=jnp.float32
    )
    return (row_max, totals, summed)


def block_grads(query_rows, key_rows, value_rows, grad_rows, usable, log_norm, row_delta, scaling):
    scores = (
        jnp.einsum("qd,kd->qk", query_rows, key_rows, preferred_element_type=jnp.float32) * scaling
    )
    allowed = usable[:, None] & usable[None, :]
    probs = jnp.where(allowed, jnp.exp(scores - log_norm[:, None]), 0.0)
    results = ()
    results = results + (
        jnp.einsum(
            "qk,qd->kd", probs.astype(jnp.bfloat16), grad_rows, preferred_element_type=jnp.float32
        ),
    )
    grad_probs = jnp.einsum("qd,kd->qk", grad_rows, value_rows, preferred_element_type=jnp.float32)
    grad_scores = (probs * (grad_probs - row_delta[:, None])).astype(jnp.bfloat16)
    grad_query = (
        jnp.einsum("qk,kd->qd", grad_scores, key_rows, preferred_element_type=jnp.float32) * scaling
    )
    grad_key = (
        jnp.einsum("qk,qd->kd", grad_scores, query_rows, preferred_element_type=jnp.float32)
        * scaling
    )
    results = results + (grad_query, grad_key)
    return results


def pick_rows(input_matrix, start_shift):
    if input_matrix.ndim == 1:
        reshaped_tensor = input_matrix.reshape(
            input_matrix.shape[0] // DILATION_STEP, DILATION_STEP
        )
        return lax.dynamic_index_in_dim(reshaped_tensor, start_shift, axis=1, keepdims=False)
    width = input_matrix.shape[1]
    return lax.dynamic_slice_in_dim(dense(input_matrix), start_shift * width, width, 1)


def spread_rows(input_matrix, start_shift, filler):
    picked_index = jnp.arange(DILATION_STEP, dtype=jnp.int32) == start_shift
    return jnp.where(picked_index[None, :], input_matrix[:, None], filler).reshape(-1)


def place_cols(input_matrix, start_shift):
    width = input_matrix.shape[1]
    picked_block = jnp.arange(DILATION_STEP * width, dtype=jnp.int32) // width == start_shift
    return jnp.where(picked_block[None, :], jnp.tile(input_matrix, (1, DILATION_STEP)), 0.0)


def by_segment(input_matrix):
    return input_matrix.reshape((input_matrix.shape[0] // SEG, SEG) + input_matrix.shape[1:])


def head_stats(query, key, value, usable, start_shift, scaling):
    seq_rows = query.shape[0]

    def segment_stats(pieces):
        row_max, totals, summed = block_stats(pieces[0], pieces[1], pieces[2], pieces[3], scaling)
        return (row_max, totals, dense(summed))

    max_w, sum_w, acc_w = lax.map(
        segment_stats, (by_segment(query), by_segment(key), by_segment(value), by_segment(usable))
    )
    usable_d = pick_rows(usable, start_shift)
    max_d, sum_d, acc_d = block_stats(
        pick_rows(query, start_shift),
        pick_rows(key, start_shift),
        pick_rows(value, start_shift),
        usable_d,
        scaling,
    )
    return (
        max_w.reshape(seq_rows),
        sum_w.reshape(seq_rows),
        acc_w.reshape(seq_rows // DILATION_STEP, -1),
        spread_rows(max_d, start_shift, NEG),
        spread_rows(sum_d, start_shift, 0.0),
        place_cols(acc_d, start_shift),
    )


def normalizer(statistics, grad, usable):
    max_w, sum_w, acc_w, max_d, sum_d, acc_d = statistics
    largest = jnp.maximum(max_w, max_d)
    totals = sum_w * jnp.exp(max_w - largest) + sum_d * jnp.exp(max_d - largest)
    log_norm = jnp.where(usable, largest + jnp.log(jnp.where(usable, totals, 1.0)), 0.0)
    weight_window = jnp.repeat(jnp.exp(max_w - log_norm).reshape(-1, DILATION_STEP), HD, axis=1)
    weight_dilated = jnp.repeat(jnp.exp(max_d - log_norm).reshape(-1, DILATION_STEP), HD, axis=1)
    attended = weight_window * acc_w + weight_dilated * acc_d
    products = dense(grad).astype(jnp.float32) * attended
    row_delta = jnp.sum(products.reshape(products.shape[0], DILATION_STEP, HD), axis=2).reshape(-1)
    return (log_norm, row_delta)


def head_grads(query, key, value, grad, usable, start_shift, log_norm, row_delta, scaling):
    seq_rows = query.shape[0]

    def segment_grads(pieces):
        parts_out = block_grads(
            pieces[0], pieces[1], pieces[2], pieces[3], pieces[4], pieces[5], pieces[6], scaling
        )
        return tuple((dense(entry) for entry in parts_out))

    window = lax.map(
        segment_grads,
        (
            by_segment(query),
            by_segment(key),
            by_segment(value),
            by_segment(grad),
            by_segment(usable),
            by_segment(log_norm),
            by_segment(row_delta),
        ),
    )
    dilated = block_grads(
        pick_rows(query, start_shift),
        pick_rows(key, start_shift),
        pick_rows(value, start_shift),
        pick_rows(grad, start_shift),
        pick_rows(usable, start_shift),
        pick_rows(log_norm, start_shift),
        pick_rows(row_delta, start_shift),
        scaling,
    )
    return tuple(
        (
            first.reshape(seq_rows // DILATION_STEP, -1) + place_cols(second, start_shift)
            for first, second in zip(window, dilated)
        )
    )


def columns(input_matrix, local_head):
    return input_matrix[:, local_head * HD : (local_head + 1) * HD]


def join_heads(dense_list, seq_rows):
    pieces = [entry.reshape(seq_rows, HD) for entry in dense_list]
    if len(pieces) == 1:
        return pieces[0].astype(jnp.bfloat16)
    return jnp.concatenate(pieces, axis=1).astype(jnp.bfloat16)


def on_device(queries, keys, values, out_grad, tissue, valid_count):
    tissue_flags = lax.all_gather(tissue, "seq", axis=0, tiled=True)
    head_queries, head_keys, head_values, head_grad = (
        lax.all_to_all(queries, "seq", split_axis=1, concat_axis=0, tiled=True),
        lax.all_to_all(keys, "seq", split_axis=1, concat_axis=0, tiled=True),
        lax.all_to_all(values, "seq", split_axis=1, concat_axis=0, tiled=True),
        lax.all_to_all(out_grad, "seq", split_axis=1, concat_axis=0, tiled=True),
    )
    seq_rows = head_queries.shape[0]
    heads_here = head_queries.shape[1] // HD
    block_rows = seq_rows // tissue_flags.shape[0]
    row_index = jnp.arange(seq_rows, dtype=jnp.int32)
    tissue_rows = jnp.broadcast_to(
        tissue_flags[:, None] == 1, (tissue_flags.shape[0], block_rows)
    ).reshape(seq_rows)
    usable = (row_index < valid_count[0]) & tissue_rows
    scaling = 1.0 / math.sqrt(HD)
    leading_head = lax.axis_index("seq") * heads_here
    start_shifts = [(leading_head + local_head) % DILATION_STEP for local_head in range(heads_here)]
    statistics = [
        head_stats(
            columns(head_queries, local_head),
            columns(head_keys, local_head),
            columns(head_values, local_head),
            usable,
            start_shifts[local_head],
            scaling,
        )
        for local_head in range(heads_here)
    ]
    normalized = [
        normalizer(statistics[local_head], columns(head_grad, local_head), usable)
        for local_head in range(heads_here)
    ]

    def grads_of(local_head):
        return head_grads(
            columns(head_queries, local_head),
            columns(head_keys, local_head),
            columns(head_values, local_head),
            columns(head_grad, local_head),
            usable,
            start_shifts[local_head],
            normalized[local_head][0],
            normalized[local_head][1],
            scaling,
        )

    results = [grads_of(local_head) for local_head in range(heads_here)]
    value_part = join_heads([entry[0] for entry in results], seq_rows)
    query_part = join_heads([entry[1] for entry in results], seq_rows)
    key_part = join_heads([entry[2] for entry in results], seq_rows)
    grad_query, grad_key, grad_value = (
        lax.all_to_all(query_part, "seq", split_axis=0, concat_axis=1, tiled=True),
        lax.all_to_all(key_part, "seq", split_axis=0, concat_axis=1, tiled=True),
        lax.all_to_all(value_part, "seq", split_axis=0, concat_axis=1, tiled=True),
    )
    return (grad_query, grad_key, grad_value)


PAIR = 2 * HD
QB = 256
FLOOR = -1e29
PEER_ORDER = (1, 6, 7, 2, 3, 4, 5)
CORE_ORDER = (6, 2, 4, 7, 3, 5)
ONCE = 8


def log2_pieces():
    left, pieces = math.log(2.0), []
    for _ in range(3):
        piece = float(np.asarray(left, jnp.bfloat16))
        pieces.append(piece)
        left -= piece
    return pieces


def partner(me, step):
    other = me
    for bit in (1, 2, 4):
        other = other + bit * (1 - 2 * ((me // bit) % 2)) * ((step // bit) % 2)
    return other


def nt_dot(a, b):
    return lax.dot_general(a, b, (((1,), (1,)), ((), ())), preferred_element_type=jnp.float32)


def fused_kernel(
    n,
    q_ref,
    k_ref,
    v_ref,
    g_ref,
    tissue_ref,
    count_ref,
    grads_ref,
    buf,
    flags,
    key_side,
    query_side,
    key_cols,
    sums,
    res,
    arrive,
    once,
    tissue_here,
):
    me = lax.axis_index("seq")
    local = q_ref.shape[0]
    rows = n * local
    pairs = buf.shape[0]
    width = pairs * PAIR
    chip = QB // local
    scaling = 1.0 / math.sqrt(HD)
    peers = [partner(me, step) for step in range(n)]

    def rows_of(device):
        return pl.ds(pl.multiple_of(device * local, local), local)

    def cols_of(device, pair):
        return pl.ds(pl.multiple_of(device * width + pair * PAIR, PAIR), PAIR)

    def remote(src, dst, send, recv, device):
        return pltpu.make_async_remote_copy(
            src_ref=src,
            dst_ref=dst,
            send_sem=send,
            recv_sem=recv,
            device_id={"seq": device},
            device_id_type=pl.DeviceIdType.MESH,
        )

    barrier = pltpu.get_barrier_semaphore()
    for step in range(1, n):
        pl.semaphore_signal(
            barrier, inc=1, device_id={"seq": peers[step]}, device_id_type=pl.DeviceIdType.MESH
        )

    flag_send, flag_recv, in_send, out_send, out_recv, own_in, own_out, small = (
        once.at[index] for index in range(ONCE)
    )
    pl.semaphore_wait(barrier, n - 1)

    ins = (k_ref, v_ref, q_ref, g_ref)

    def send_in(pair, group):
        for step in PEER_ORDER:
            for which in range(2 * group, 2 * group + 2):
                remote(
                    ins[which].at[:, cols_of(peers[step], pair)],
                    buf.at[pair, which, rows_of(me), :],
                    in_send,
                    arrive.at[pair, 1 + step // chip if group else 0],
                    peers[step],
                ).start()

    send_in(0, 0)
    tissue_copy = pltpu.make_async_copy(tissue_ref, tissue_here, small)
    tissue_copy.start()
    for pair in range(pairs):
        for which in range(4):
            pltpu.make_async_copy(
                ins[which].at[:, cols_of(me, pair)], buf.at[pair, which, rows_of(me), :], own_in
            ).start()
    tissue_copy.wait()
    spot = lax.broadcasted_iota(jnp.int32, flags.shape[1:], 1)
    blocks_here = tissue_here.shape[0]
    tissue = jnp.zeros_like(spot)
    for block in range(blocks_here):
        tissue = jnp.where(spot // (local // blocks_here) == block, tissue_here[block], tissue)
    usable = (me * local + spot < count_ref[0]) & (tissue == 1)
    flags[me] = usable.astype(jnp.float32)
    for step in PEER_ORDER:
        remote(
            flags.at[me, pl.ds(0, 1)], flags.at[me, pl.ds(0, 1)], flag_send, flag_recv, peers[step]
        ).start()
    send_in(0, 1)
    for pair in range(1, pairs):
        send_in(pair, 0)
        send_in(pair, 1)

    def landed(ref, sem):
        remote(ref, ref, in_send, sem, peers[1]).wait_recv()

    def left(ref, sem):
        remote(ref, ref, sem, out_recv, peers[1]).wait_send()

    theirs = pl.ds(0, rows - local)
    mine = buf.at[:, :, pl.ds(0, local), :]
    pltpu.make_async_copy(mine, mine, own_in).wait()
    landed(flags.at[0, pl.ds(0, n - 1)], flag_recv)
    lane = lax.broadcasted_iota(jnp.int32, (local, PAIR), 1)
    residue = lax.broadcasted_iota(jnp.int32, (local, PAIR), 0) % DILATION_STEP
    pieces = log2_pieces()
    piece = jnp.where(lane < 8, pieces[0], jnp.where(lane < 16, pieces[1], pieces[2]))
    same = (lane < 24) & (lane % DILATION_STEP == residue)
    for block in range(n):
        flag = jnp.transpose(jnp.broadcast_to(flags[block, 0:1, :], (local, PAIR)))
        off = (1.0 - flag) * NEG
        side = jnp.where(lane == 24, off, jnp.where(lane == 25, 1.0, jnp.where(same, piece, 0.0)))
        here = pl.ds(block * local, local)
        for pair in range(pairs):
            key_side[pair, here, PAIR:] = side.astype(jnp.bfloat16)
        for head in range(2 * pairs):
            shift = (me * 2 * pairs + head) % DILATION_STEP
            chosen = same & (lane % DILATION_STEP == shift)
            side = jnp.where(
                lane == 24, 1.0, jnp.where(lane == 25, off, jnp.where(chosen, 1.0, 0.0))
            )
            query_side[head, here, :] = side.astype(jnp.bfloat16)

    half = lax.broadcasted_iota(jnp.int32, (QB, PAIR), 1) // HD

    def send_out(pair, which, device):
        remote(
            res.at[pair, which, rows_of(device), :],
            grads_ref.at[which, :, cols_of(me, pair)],
            out_send,
            out_recv,
            device,
        ).start()

    for pair in range(pairs):
        landed(buf.at[pair, pl.ds(0, 2), theirs, :], arrive.at[pair, 0])
        key_side[pair, :, :PAIR] = buf[pair, 0]
        key_cols[...] = jnp.transpose(buf[pair, 0].astype(jnp.float32)).astype(jnp.bfloat16)
        sums[...] = jnp.zeros_like(sums)

        def query_block(index, carry, pair=pair):
            far = (n // chip - index) % (n // chip) if pair == 0 else n // chip - 1 - index
            for count, here in ((chip - 1, far == 0), (chip, far > 0)):

                @pl.when(here)
                def _(count=count):
                    these = pl.ds(0, count * local)
                    landed(buf.at[pair, pl.ds(2, 2), these, :], arrive.at[pair, 1 + far])

            first = partner(me - me % chip, far * chip)
            here = pl.ds(pl.multiple_of(first * local, QB), QB)
            query = buf[pair, 2, here, :].astype(jnp.float32) * scaling
            grad = buf[pair, 3, here, :].astype(jnp.float32)
            columns_out = []
            for side in range(2):
                query_h = jnp.where(half == side, query, 0.0).astype(jnp.bfloat16)
                grad_h = jnp.where(half == side, grad, 0.0).astype(jnp.bfloat16)
                extended = jnp.concatenate(
                    [query_h, query_side[2 * pair + side, here, :]], axis=1
                )
                score = nt_dot(key_side[pair], extended)
                grad_prob = nt_dot(buf[pair, 1], grad_h)
                top = jnp.maximum(jnp.max(score, axis=0, keepdims=True), FLOOR)
                weight = jnp.exp(score - top)
                total = jnp.maximum(jnp.sum(weight, axis=0, keepdims=True), 1.0)
                inverse = 1.0 / total
                delta = jnp.sum(weight * grad_prob, axis=0, keepdims=True) * inverse
                prob = weight * inverse
                dscore = (prob * (grad_prob - delta)).astype(jnp.bfloat16)
                sums[0] += jnp.dot(dscore, query_h, preferred_element_type=jnp.float32)
                sums[1] += jnp.dot(
                    prob.astype(jnp.bfloat16), grad_h, preferred_element_type=jnp.float32
                )
                columns_out.append(
                    jnp.dot(
                        key_cols[side * HD : (side + 1) * HD, :],
                        dscore,
                        preferred_element_type=jnp.float32,
                    )
                )
            grad_query = jnp.transpose(jnp.concatenate(columns_out, axis=0)) * scaling
            res[pair, 0, here, :] = grad_query.astype(jnp.bfloat16)
            for part in range(chip):
                step = far * chip + part

                def leaves(step=step):
                    send_out(pair, 0, partner(me, step))

                if part == 0:
                    pl.when(step > 0)(leaves)
                else:
                    leaves()
            return carry

        lax.fori_loop(0, rows // QB, query_block, 0)
        res[pair, 1] = sums[0].astype(jnp.bfloat16)
        res[pair, 2] = sums[1].astype(jnp.bfloat16)
        send_out(pair, pl.ds(1, 2), peers[1])
        for step in CORE_ORDER:
            swap = (me % 2) * (1 - 2 * (step % 2))
            send_out(pair, pl.ds(1, 2), partner(me, step + swap))
        pltpu.make_async_copy(
            res.at[pair, :, rows_of(me), :], grads_ref.at[:, :, cols_of(me, pair)], own_out
        ).start()
    left(flags.at[0, pl.ds(0, n - 1)], flag_send)
    left(buf.at[:, :, theirs, :], in_send)
    mine = res.at[:, :, pl.ds(0, local), :]
    pltpu.make_async_copy(mine, mine, own_out).wait()
    left(res.at[:, :, theirs, :], out_send)
    landed(res.at[:, :, theirs, :], out_recv)


def write_kernel(grads_ref, dq_ref, dk_ref, dv_ref, sem):
    copies = [
        pltpu.make_async_copy(grads_ref.at[which], out, sem.at[0])
        for which, out in enumerate((dq_ref, dk_ref, dv_ref))
    ]
    for copy in copies:
        copy.start()
    for copy in copies:
        copy.wait()


def on_device_fused(n, queries, keys, values, out_grad, tissue, valid_count):
    local, features = queries.shape
    rows = n * local
    pairs = features // n // PAIR
    hbm = pl.BlockSpec(memory_space=pltpu.HBM)
    vmem = pl.BlockSpec(memory_space=pltpu.VMEM)
    smem = pl.BlockSpec(memory_space=pltpu.SMEM)
    dma = pltpu.SemaphoreType.DMA
    grads = pl.pallas_call(
        functools.partial(fused_kernel, n),
        out_shape=pltpu.VMEM((3, local, features), jnp.bfloat16),
        in_specs=[hbm] * 5 + [smem],
        out_specs=vmem,
        scratch_shapes=[
            pltpu.VMEM((pairs, 4, rows, PAIR), jnp.bfloat16),
            pltpu.VMEM((n, 8, local), jnp.float32),
            pltpu.VMEM((pairs, rows, 2 * PAIR), jnp.bfloat16),
            pltpu.VMEM((2 * pairs, rows, PAIR), jnp.bfloat16),
            pltpu.VMEM((PAIR, rows), jnp.bfloat16),
            pltpu.VMEM((2, rows, PAIR), jnp.float32),
            pltpu.VMEM((pairs, 3, rows, PAIR), jnp.bfloat16),
            dma((pairs, 1 + rows // QB)),
            dma((ONCE,)),
            pltpu.SMEM(tissue.shape, jnp.int32),
        ],
        compiler_params=pltpu.CompilerParams(
            collective_id=0, has_side_effects=True, vmem_limit_bytes=48 * 2**20
        ),
        name="attention_backward",
    )(
        *(
            pltpu.with_memory_space_constraint(entry, pltpu.HBM)
            for entry in (queries, keys, values, out_grad, tissue)
        ),
        valid_count,
    )
    return tuple(
        pl.pallas_call(
            write_kernel,
            out_shape=[jax.ShapeDtypeStruct((local, features), jnp.bfloat16)] * 3,
            in_specs=[vmem],
            out_specs=[hbm] * 3,
            scratch_shapes=[dma((1,))],
            compiler_params=pltpu.CompilerParams(vmem_limit_bytes=4 * 2**20),
            name="write_gradients",
        )(grads)
    )


def solution(mesh):
    in_specs = (
        P(("slide", "seq"), None),
        P(("slide", "seq"), None),
        P(("slide", "seq"), None),
        P(("slide", "seq"), None),
        P(("slide", "seq")),
        P("slide"),
    )
    out_specs = (P(("slide", "seq"), None), P(("slide", "seq"), None), P(("slide", "seq"), None))
    n = mesh.shape["seq"]

    def body(queries, keys, values, out_grad, tissue, valid_count):
        arguments = (queries, keys, values, out_grad, tissue, valid_count)
        local, features = queries.shape
        if n == 8 and local == PAIR and n * local == SEG and features % (n * PAIR) == 0:
            return on_device_fused(n, *arguments)
        return on_device(*arguments)

    return jax.shard_map(
        body, mesh=mesh, in_specs=in_specs, out_specs=out_specs, check_vma=False
    )
```

```python
import functools
import math

import jax
import jax.numpy as jnp
import numpy as np
from jax import lax
from jax.experimental import pallas as pl
from jax.experimental.pallas import tpu as pltpu
from jax.sharding import PartitionSpec as P

HD = 64
SEG = 1024
DILATION_STEP = 8


NEG = -1e30


def dense(input_matrix):
    return input_matrix.reshape(
        input_matrix.shape[0] // DILATION_STEP, DILATION_STEP * input_matrix.shape[1]
    )


def block_stats(query_rows, key_rows, value_rows, usable, scaling):
    scores = (
        jnp.einsum("qd,kd->qk", query_rows, key_rows, preferred_element_type=jnp.float32) * scaling
    )
    allowed = usable[:, None] & usable[None, :]
    row_max = jnp.max(jnp.where(allowed, scores, NEG), axis=1)
    weights = jnp.where(allowed, jnp.exp(scores - row_max[:, None]), 0.0)
    totals = jnp.sum(weights, axis=1)
    summed = jnp.einsum(
        "qk,kd->qd", weights.astype(jnp.bfloat16), value_rows, preferred_element_type=jnp.float32
    )
    return (row_max, totals, summed)


def block_grads(query_rows, key_rows, value_rows, grad_rows, usable, log_norm, row_delta, scaling):
    scores = (
        jnp.einsum("qd,kd->qk", query_rows, key_rows, preferred_element_type=jnp.float32) * scaling
    )
    allowed = usable[:, None] & usable[None, :]
    probs = jnp.where(allowed, jnp.exp(scores - log_norm[:, None]), 0.0)
    results = ()
    results = results + (
        jnp.einsum(
            "qk,qd->kd", probs.astype(jnp.bfloat16), grad_rows, preferred_element_type=jnp.float32
        ),
    )
    grad_probs = jnp.einsum("qd,kd->qk", grad_rows, value_rows, preferred_element_type=jnp.float32)
    grad_scores = (probs * (grad_probs - row_delta[:, None])).astype(jnp.bfloat16)
    grad_query = (
        jnp.einsum("qk,kd->qd", grad_scores, key_rows, preferred_element_type=jnp.float32) * scaling
    )
    grad_key = (
        jnp.einsum("qk,qd->kd", grad_scores, query_rows, preferred_element_type=jnp.float32)
        * scaling
    )
    results = results + (grad_query, grad_key)
    return results


def pick_rows(input_matrix, start_shift):
    if input_matrix.ndim == 1:
        reshaped_tensor = input_matrix.reshape(
            input_matrix.shape[0] // DILATION_STEP, DILATION_STEP
        )
        return lax.dynamic_index_in_dim(reshaped_tensor, start_shift, axis=1, keepdims=False)
    width = input_matrix.shape[1]
    return lax.dynamic_slice_in_dim(dense(input_matrix), start_shift * width, width, 1)


def spread_rows(input_matrix, start_shift, filler):
    picked_index = jnp.arange(DILATION_STEP, dtype=jnp.int32) == start_shift
    return jnp.where(picked_index[None, :], input_matrix[:, None], filler).reshape(-1)


def place_cols(input_matrix, start_shift):
    width = input_matrix.shape[1]
    picked_block = jnp.arange(DILATION_STEP * width, dtype=jnp.int32) // width == start_shift
    return jnp.where(picked_block[None, :], jnp.tile(input_matrix, (1, DILATION_STEP)), 0.0)


def by_segment(input_matrix):
    return input_matrix.reshape((input_matrix.shape[0] // SEG, SEG) + input_matrix.shape[1:])


def head_stats(query, key, value, usable, start_shift, scaling):
    seq_rows = query.shape[0]

    def segment_stats(pieces):
        row_max, totals, summed = block_stats(pieces[0], pieces[1], pieces[2], pieces[3], scaling)
        return (row_max, totals, dense(summed))

    max_w, sum_w, acc_w = lax.map(
        segment_stats, (by_segment(query), by_segment(key), by_segment(value), by_segment(usable))
    )
    usable_d = pick_rows(usable, start_shift)
    max_d, sum_d, acc_d = block_stats(
        pick_rows(query, start_shift),
        pick_rows(key, start_shift),
        pick_rows(value, start_shift),
        usable_d,
        scaling,
    )
    return (
        max_w.reshape(seq_rows),
        sum_w.reshape(seq_rows),
        acc_w.reshape(seq_rows // DILATION_STEP, -1),
        spread_rows(max_d, start_shift, NEG),
        spread_rows(sum_d, start_shift, 0.0),
        place_cols(acc_d, start_shift),
    )


def normalizer(statistics, grad, usable):
    max_w, sum_w, acc_w, max_d, sum_d, acc_d = statistics
    largest = jnp.maximum(max_w, max_d)
    totals = sum_w * jnp.exp(max_w - largest) + sum_d * jnp.exp(max_d - largest)
    log_norm = jnp.where(usable, largest + jnp.log(jnp.where(usable, totals, 1.0)), 0.0)
    weight_window = jnp.repeat(jnp.exp(max_w - log_norm).reshape(-1, DILATION_STEP), HD, axis=1)
    weight_dilated = jnp.repeat(jnp.exp(max_d - log_norm).reshape(-1, DILATION_STEP), HD, axis=1)
    attended = weight_window * acc_w + weight_dilated * acc_d
    products = dense(grad).astype(jnp.float32) * attended
    row_delta = jnp.sum(products.reshape(products.shape[0], DILATION_STEP, HD), axis=2).reshape(-1)
    return (log_norm, row_delta)


def head_grads(query, key, value, grad, usable, start_shift, log_norm, row_delta, scaling):
    seq_rows = query.shape[0]

    def segment_grads(pieces):
        parts_out = block_grads(
            pieces[0], pieces[1], pieces[2], pieces[3], pieces[4], pieces[5], pieces[6], scaling
        )
        return tuple((dense(entry) for entry in parts_out))

    window = lax.map(
        segment_grads,
        (
            by_segment(query),
            by_segment(key),
            by_segment(value),
            by_segment(grad),
            by_segment(usable),
            by_segment(log_norm),
            by_segment(row_delta),
        ),
    )
    dilated = block_grads(
        pick_rows(query, start_shift),
        pick_rows(key, start_shift),
        pick_rows(value, start_shift),
        pick_rows(grad, start_shift),
        pick_rows(usable, start_shift),
        pick_rows(log_norm, start_shift),
        pick_rows(row_delta, start_shift),
        scaling,
    )
    return tuple(
        (
            first.reshape(seq_rows // DILATION_STEP, -1) + place_cols(second, start_shift)
            for first, second in zip(window, dilated)
        )
    )


def columns(input_matrix, local_head):
    return input_matrix[:, local_head * HD : (local_head + 1) * HD]


def join_heads(dense_list, seq_rows):
    pieces = [entry.reshape(seq_rows, HD) for entry in dense_list]
    if len(pieces) == 1:
        return pieces[0].astype(jnp.bfloat16)
    return jnp.concatenate(pieces, axis=1).astype(jnp.bfloat16)


def on_device(queries, keys, values, out_grad, tissue, valid_count):
    tissue_flags = lax.all_gather(tissue, "seq", axis=0, tiled=True)
    head_queries, head_keys, head_values, head_grad = (
        lax.all_to_all(queries, "seq", split_axis=1, concat_axis=0, tiled=True),
        lax.all_to_all(keys, "seq", split_axis=1, concat_axis=0, tiled=True),
        lax.all_to_all(values, "seq", split_axis=1, concat_axis=0, tiled=True),
        lax.all_to_all(out_grad, "seq", split_axis=1, concat_axis=0, tiled=True),
    )
    seq_rows = head_queries.shape[0]
    heads_here = head_queries.shape[1] // HD
    block_rows = seq_rows // tissue_flags.shape[0]
    row_index = jnp.arange(seq_rows, dtype=jnp.int32)
    tissue_rows = jnp.broadcast_to(
        tissue_flags[:, None] == 1, (tissue_flags.shape[0], block_rows)
    ).reshape(seq_rows)
    usable = (row_index < valid_count[0]) & tissue_rows
    scaling = 1.0 / math.sqrt(HD)
    leading_head = lax.axis_index("seq") * heads_here
    start_shifts = [(leading_head + local_head) % DILATION_STEP for local_head in range(heads_here)]
    statistics = [
        head_stats(
            columns(head_queries, local_head),
            columns(head_keys, local_head),
            columns(head_values, local_head),
            usable,
            start_shifts[local_head],
            scaling,
        )
        for local_head in range(heads_here)
    ]
    normalized = [
        normalizer(statistics[local_head], columns(head_grad, local_head), usable)
        for local_head in range(heads_here)
    ]

    def grads_of(local_head):
        return head_grads(
            columns(head_queries, local_head),
            columns(head_keys, local_head),
            columns(head_values, local_head),
            columns(head_grad, local_head),
            usable,
            start_shifts[local_head],
            normalized[local_head][0],
            normalized[local_head][1],
            scaling,
        )

    results = [grads_of(local_head) for local_head in range(heads_here)]
    value_part = join_heads([entry[0] for entry in results], seq_rows)
    query_part = join_heads([entry[1] for entry in results], seq_rows)
    key_part = join_heads([entry[2] for entry in results], seq_rows)
    grad_query, grad_key, grad_value = (
        lax.all_to_all(query_part, "seq", split_axis=0, concat_axis=1, tiled=True),
        lax.all_to_all(key_part, "seq", split_axis=0, concat_axis=1, tiled=True),
        lax.all_to_all(value_part, "seq", split_axis=0, concat_axis=1, tiled=True),
    )
    return (grad_query, grad_key, grad_value)


PAIR = 2 * HD
QB = 256
FLOOR = -1e29
PEER_ORDER = (1, 6, 7, 2, 3, 4, 5)
LAST_ORDER = ((0, 0), (0, 1), (1, 0), (2, 0), (1, 1), (2, 1))
ONCE = 8


def log2_pieces():
    left, pieces = math.log(2.0), []
    for _ in range(3):
        piece = float(np.asarray(left, jnp.bfloat16))
        pieces.append(piece)
        left -= piece
    return pieces


def partner(me, step):
    other = me
    for bit in (1, 2, 4):
        other = other + bit * (1 - 2 * ((me // bit) % 2)) * ((step // bit) % 2)
    return other


def nt_dot(a, b):
    return lax.dot_general(a, b, (((1,), (1,)), ((), ())), preferred_element_type=jnp.float32)


def fused_kernel(
    n,
    q_ref,
    k_ref,
    v_ref,
    g_ref,
    tissue_ref,
    count_ref,
    grads_ref,
    buf,
    flags,
    key_side,
    query_side,
    key_cols,
    sums,
    res,
    arrive,
    once,
    tissue_here,
):
    me = lax.axis_index("seq")
    local = q_ref.shape[0]
    rows = n * local
    pairs = buf.shape[0]
    width = pairs * PAIR
    chip = QB // local
    scaling = 1.0 / math.sqrt(HD)
    peers = [partner(me, step) for step in range(n)]

    def rows_of(device):
        return pl.ds(pl.multiple_of(device * local, local), local)

    def cols_of(device, pair):
        return pl.ds(pl.multiple_of(device * width + pair * PAIR, PAIR), PAIR)

    def remote(src, dst, send, recv, device):
        return pltpu.make_async_remote_copy(
            src_ref=src,
            dst_ref=dst,
            send_sem=send,
            recv_sem=recv,
            device_id={"seq": device},
            device_id_type=pl.DeviceIdType.MESH,
        )

    barrier = pltpu.get_barrier_semaphore()
    for step in range(1, n):
        pl.semaphore_signal(
            barrier, inc=1, device_id={"seq": peers[step]}, device_id_type=pl.DeviceIdType.MESH
        )

    flag_send, flag_recv, in_send, out_send, out_recv, own_in, own_out, small = (
        once.at[index] for index in range(ONCE)
    )
    pl.semaphore_wait(barrier, n - 1)

    ins = (k_ref, v_ref, q_ref, g_ref)

    def send_in(pair, group):
        for step in PEER_ORDER:
            for which in range(2 * group, 2 * group + 2):
                remote(
                    ins[which].at[:, cols_of(peers[step], pair)],
                    buf.at[pair, which, rows_of(me), :],
                    in_send,
                    arrive.at[pair, 1 + step // chip if group else 0],
                    peers[step],
                ).start()

    send_in(0, 0)
    tissue_copy = pltpu.make_async_copy(tissue_ref, tissue_here, small)
    tissue_copy.start()
    for pair in range(pairs):
        for which in range(4):
            pltpu.make_async_copy(
                ins[which].at[:, cols_of(me, pair)], buf.at[pair, which, rows_of(me), :], own_in
            ).start()
    tissue_copy.wait()
    spot = lax.broadcasted_iota(jnp.int32, flags.shape[1:], 1)
    blocks_here = tissue_here.shape[0]
    tissue = jnp.zeros_like(spot)
    for block in range(blocks_here):
        tissue = jnp.where(spot // (local // blocks_here) == block, tissue_here[block], tissue)
    usable = (me * local + spot < count_ref[0]) & (tissue == 1)
    flags[me] = usable.astype(jnp.float32)
    for step in PEER_ORDER:
        remote(
            flags.at[me, pl.ds(0, 1)], flags.at[me, pl.ds(0, 1)], flag_send, flag_recv, peers[step]
        ).start()
    send_in(0, 1)
    for pair in range(1, pairs):
        send_in(pair, 0)
        send_in(pair, 1)

    def landed(ref, sem):
        remote(ref, ref, in_send, sem, peers[1]).wait_recv()

    def left(ref, sem):
        remote(ref, ref, sem, out_recv, peers[1]).wait_send()

    theirs = pl.ds(0, rows - local)
    mine = buf.at[:, :, pl.ds(0, local), :]
    pltpu.make_async_copy(mine, mine, own_in).wait()
    landed(flags.at[0, pl.ds(0, n - 1)], flag_recv)
    lane = lax.broadcasted_iota(jnp.int32, (local, PAIR), 1)
    residue = lax.broadcasted_iota(jnp.int32, (local, PAIR), 0) % DILATION_STEP
    pieces = log2_pieces()
    piece = jnp.where(lane < 8, pieces[0], jnp.where(lane < 16, pieces[1], pieces[2]))
    same = (lane < 24) & (lane % DILATION_STEP == residue)
    for block in range(n):
        flag = jnp.transpose(jnp.broadcast_to(flags[block, 0:1, :], (local, PAIR)))
        off = (1.0 - flag) * NEG
        side = jnp.where(lane == 24, off, jnp.where(lane == 25, 1.0, jnp.where(same, piece, 0.0)))
        here = pl.ds(block * local, local)
        for pair in range(pairs):
            key_side[pair, here, PAIR:] = side.astype(jnp.bfloat16)
        for head in range(2 * pairs):
            shift = (me * 2 * pairs + head) % DILATION_STEP
            chosen = same & (lane % DILATION_STEP == shift)
            side = jnp.where(
                lane == 24, 1.0, jnp.where(lane == 25, off, jnp.where(chosen, 1.0, 0.0))
            )
            query_side[head, here, :] = side.astype(jnp.bfloat16)

    half = lax.broadcasted_iota(jnp.int32, (QB, PAIR), 1) // HD

    def send_out(pair, which, device):
        remote(
            res.at[pair, which, rows_of(device), :],
            grads_ref.at[which, :, cols_of(me, pair)],
            out_send,
            out_recv,
            device,
        ).start()

    for pair in range(pairs):
        landed(buf.at[pair, pl.ds(0, 2), theirs, :], arrive.at[pair, 0])
        key_side[pair, :, :PAIR] = buf[pair, 0]
        key_cols[...] = jnp.transpose(buf[pair, 0].astype(jnp.float32)).astype(jnp.bfloat16)
        sums[...] = jnp.zeros_like(sums)

        def query_block(index, carry, pair=pair):
            far = (n // chip - index) % (n // chip) if pair == 0 else n // chip - 1 - index
            for count, here in ((chip - 1, far == 0), (chip, far > 0)):

                @pl.when(here)
                def _(count=count):
                    these = pl.ds(0, count * local)
                    landed(buf.at[pair, pl.ds(2, 2), these, :], arrive.at[pair, 1 + far])

            first = partner(me - me % chip, far * chip)
            here = pl.ds(pl.multiple_of(first * local, QB), QB)
            query = buf[pair, 2, here, :].astype(jnp.float32) * scaling
            grad = buf[pair, 3, here, :].astype(jnp.float32)
            columns_out = []
            for side in range(2):
                query_h = jnp.where(half == side, query, 0.0).astype(jnp.bfloat16)
                grad_h = jnp.where(half == side, grad, 0.0).astype(jnp.bfloat16)
                extended = jnp.concatenate(
                    [query_h, query_side[2 * pair + side, here, :]], axis=1
                )
                score = nt_dot(key_side[pair], extended)
                grad_prob = nt_dot(buf[pair, 1], grad_h)
                top = jnp.maximum(jnp.max(score, axis=0, keepdims=True), FLOOR)
                weight = jnp.exp(score - top)
                total = jnp.maximum(jnp.sum(weight, axis=0, keepdims=True), 1.0)
                inverse = 1.0 / total
                delta = jnp.sum(weight * grad_prob, axis=0, keepdims=True) * inverse
                prob = weight * inverse
                dscore = (prob * (grad_prob - delta)).astype(jnp.bfloat16)
                sums[0] += jnp.dot(dscore, query_h, preferred_element_type=jnp.float32)
                sums[1] += jnp.dot(
                    prob.astype(jnp.bfloat16), grad_h, preferred_element_type=jnp.float32
                )
                columns_out.append(
                    jnp.dot(
                        key_cols[side * HD : (side + 1) * HD, :],
                        dscore,
                        preferred_element_type=jnp.float32,
                    )
                )
            grad_query = jnp.transpose(jnp.concatenate(columns_out, axis=0)) * scaling
            res[pair, 0, here, :] = grad_query.astype(jnp.bfloat16)
            for part in range(chip):
                step = far * chip + part

                def leaves(step=step):
                    send_out(pair, 0, partner(me, step))

                if part == 0:
                    pl.when(step > 0)(leaves)
                else:
                    leaves()
            return carry

        lax.fori_loop(0, rows // QB, query_block, 0)
        res[pair, 1] = sums[0].astype(jnp.bfloat16)
        res[pair, 2] = sums[1].astype(jnp.bfloat16)
        send_out(pair, pl.ds(1, 2), peers[1])
        here_chip = me // 2
        first = here_chip + 3 * ((3 - here_chip) // 3)
        second = 3 - 2 * (first // 3)
        order = (first, second, 6 - first - second)
        for place, core in LAST_ORDER:
            step = 2 * order[place] + core + (me % 2) * (1 - 2 * core)
            send_out(pair, pl.ds(1, 2), partner(me, step))
        pltpu.make_async_copy(
            res.at[pair, :, rows_of(me), :], grads_ref.at[:, :, cols_of(me, pair)], own_out
        ).start()
    left(flags.at[0, pl.ds(0, n - 1)], flag_send)
    left(buf.at[:, :, theirs, :], in_send)
    mine = res.at[:, :, pl.ds(0, local), :]
    pltpu.make_async_copy(mine, mine, own_out).wait()
    left(res.at[:, :, theirs, :], out_send)
    landed(res.at[:, :, theirs, :], out_recv)


def write_kernel(grads_ref, dq_ref, dk_ref, dv_ref, sem):
    copies = [
        pltpu.make_async_copy(grads_ref.at[which], out, sem.at[0])
        for which, out in enumerate((dq_ref, dk_ref, dv_ref))
    ]
    for copy in copies:
        copy.start()
    for copy in copies:
        copy.wait()


def on_device_fused(n, queries, keys, values, out_grad, tissue, valid_count):
    local, features = queries.shape
    rows = n * local
    pairs = features // n // PAIR
    hbm = pl.BlockSpec(memory_space=pltpu.HBM)
    vmem = pl.BlockSpec(memory_space=pltpu.VMEM)
    smem = pl.BlockSpec(memory_space=pltpu.SMEM)
    dma = pltpu.SemaphoreType.DMA
    grads = pl.pallas_call(
        functools.partial(fused_kernel, n),
        out_shape=pltpu.VMEM((3, local, features), jnp.bfloat16),
        in_specs=[hbm] * 5 + [smem],
        out_specs=vmem,
        scratch_shapes=[
            pltpu.VMEM((pairs, 4, rows, PAIR), jnp.bfloat16),
            pltpu.VMEM((n, 8, local), jnp.float32),
            pltpu.VMEM((pairs, rows, 2 * PAIR), jnp.bfloat16),
            pltpu.VMEM((2 * pairs, rows, PAIR), jnp.bfloat16),
            pltpu.VMEM((PAIR, rows), jnp.bfloat16),
            pltpu.VMEM((2, rows, PAIR), jnp.float32),
            pltpu.VMEM((pairs, 3, rows, PAIR), jnp.bfloat16),
            dma((pairs, 1 + rows // QB)),
            dma((ONCE,)),
            pltpu.SMEM(tissue.shape, jnp.int32),
        ],
        compiler_params=pltpu.CompilerParams(
            collective_id=0, has_side_effects=True, vmem_limit_bytes=48 * 2**20
        ),
        name="attention_backward",
    )(
        *(
            pltpu.with_memory_space_constraint(entry, pltpu.HBM)
            for entry in (queries, keys, values, out_grad, tissue)
        ),
        valid_count,
    )
    return tuple(
        pl.pallas_call(
            write_kernel,
            out_shape=[jax.ShapeDtypeStruct((local, features), jnp.bfloat16)] * 3,
            in_specs=[vmem],
            out_specs=[hbm] * 3,
            scratch_shapes=[dma((1,))],
            compiler_params=pltpu.CompilerParams(vmem_limit_bytes=4 * 2**20),
            name="write_gradients",
        )(grads)
    )


def solution(mesh):
    in_specs = (
        P(("slide", "seq"), None),
        P(("slide", "seq"), None),
        P(("slide", "seq"), None),
        P(("slide", "seq"), None),
        P(("slide", "seq")),
        P("slide"),
    )
    out_specs = (P(("slide", "seq"), None), P(("slide", "seq"), None), P(("slide", "seq"), None))
    n = mesh.shape["seq"]

    def body(queries, keys, values, out_grad, tissue, valid_count):
        arguments = (queries, keys, values, out_grad, tissue, valid_count)
        local, features = queries.shape
        if n == 8 and local == PAIR and n * local == SEG and features % (n * PAIR) == 0:
            return on_device_fused(n, *arguments)
        return on_device(*arguments)

    return jax.shard_map(
        body, mesh=mesh, in_specs=in_specs, out_specs=out_specs, check_vma=False
    )
```

```python
import functools
import math

import jax
import jax.numpy as jnp
import numpy as np
from jax import lax
from jax.experimental import pallas as pl
from jax.experimental.pallas import tpu as pltpu
from jax.sharding import PartitionSpec as P

HD = 64
SEG = 1024
DILATION_STEP = 8


NEG = -1e30


def dense(input_matrix):
    return input_matrix.reshape(
        input_matrix.shape[0] // DILATION_STEP, DILATION_STEP * input_matrix.shape[1]
    )


def block_stats(query_rows, key_rows, value_rows, usable, scaling):
    scores = (
        jnp.einsum("qd,kd->qk", query_rows, key_rows, preferred_element_type=jnp.float32) * scaling
    )
    allowed = usable[:, None] & usable[None, :]
    row_max = jnp.max(jnp.where(allowed, scores, NEG), axis=1)
    weights = jnp.where(allowed, jnp.exp(scores - row_max[:, None]), 0.0)
    totals = jnp.sum(weights, axis=1)
    summed = jnp.einsum(
        "qk,kd->qd", weights.astype(jnp.bfloat16), value_rows, preferred_element_type=jnp.float32
    )
    return (row_max, totals, summed)


def block_grads(query_rows, key_rows, value_rows, grad_rows, usable, log_norm, row_delta, scaling):
    scores = (
        jnp.einsum("qd,kd->qk", query_rows, key_rows, preferred_element_type=jnp.float32) * scaling
    )
    allowed = usable[:, None] & usable[None, :]
    probs = jnp.where(allowed, jnp.exp(scores - log_norm[:, None]), 0.0)
    results = ()
    results = results + (
        jnp.einsum(
            "qk,qd->kd", probs.astype(jnp.bfloat16), grad_rows, preferred_element_type=jnp.float32
        ),
    )
    grad_probs = jnp.einsum("qd,kd->qk", grad_rows, value_rows, preferred_element_type=jnp.float32)
    grad_scores = (probs * (grad_probs - row_delta[:, None])).astype(jnp.bfloat16)
    grad_query = (
        jnp.einsum("qk,kd->qd", grad_scores, key_rows, preferred_element_type=jnp.float32) * scaling
    )
    grad_key = (
        jnp.einsum("qk,qd->kd", grad_scores, query_rows, preferred_element_type=jnp.float32)
        * scaling
    )
    results = results + (grad_query, grad_key)
    return results


def pick_rows(input_matrix, start_shift):
    if input_matrix.ndim == 1:
        reshaped_tensor = input_matrix.reshape(
            input_matrix.shape[0] // DILATION_STEP, DILATION_STEP
        )
        return lax.dynamic_index_in_dim(reshaped_tensor, start_shift, axis=1, keepdims=False)
    width = input_matrix.shape[1]
    return lax.dynamic_slice_in_dim(dense(input_matrix), start_shift * width, width, 1)


def spread_rows(input_matrix, start_shift, filler):
    picked_index = jnp.arange(DILATION_STEP, dtype=jnp.int32) == start_shift
    return jnp.where(picked_index[None, :], input_matrix[:, None], filler).reshape(-1)


def place_cols(input_matrix, start_shift):
    width = input_matrix.shape[1]
    picked_block = jnp.arange(DILATION_STEP * width, dtype=jnp.int32) // width == start_shift
    return jnp.where(picked_block[None, :], jnp.tile(input_matrix, (1, DILATION_STEP)), 0.0)


def by_segment(input_matrix):
    return input_matrix.reshape((input_matrix.shape[0] // SEG, SEG) + input_matrix.shape[1:])


def head_stats(query, key, value, usable, start_shift, scaling):
    seq_rows = query.shape[0]

    def segment_stats(pieces):
        row_max, totals, summed = block_stats(pieces[0], pieces[1], pieces[2], pieces[3], scaling)
        return (row_max, totals, dense(summed))

    max_w, sum_w, acc_w = lax.map(
        segment_stats, (by_segment(query), by_segment(key), by_segment(value), by_segment(usable))
    )
    usable_d = pick_rows(usable, start_shift)
    max_d, sum_d, acc_d = block_stats(
        pick_rows(query, start_shift),
        pick_rows(key, start_shift),
        pick_rows(value, start_shift),
        usable_d,
        scaling,
    )
    return (
        max_w.reshape(seq_rows),
        sum_w.reshape(seq_rows),
        acc_w.reshape(seq_rows // DILATION_STEP, -1),
        spread_rows(max_d, start_shift, NEG),
        spread_rows(sum_d, start_shift, 0.0),
        place_cols(acc_d, start_shift),
    )


def normalizer(statistics, grad, usable):
    max_w, sum_w, acc_w, max_d, sum_d, acc_d = statistics
    largest = jnp.maximum(max_w, max_d)
    totals = sum_w * jnp.exp(max_w - largest) + sum_d * jnp.exp(max_d - largest)
    log_norm = jnp.where(usable, largest + jnp.log(jnp.where(usable, totals, 1.0)), 0.0)
    weight_window = jnp.repeat(jnp.exp(max_w - log_norm).reshape(-1, DILATION_STEP), HD, axis=1)
    weight_dilated = jnp.repeat(jnp.exp(max_d - log_norm).reshape(-1, DILATION_STEP), HD, axis=1)
    attended = weight_window * acc_w + weight_dilated * acc_d
    products = dense(grad).astype(jnp.float32) * attended
    row_delta = jnp.sum(products.reshape(products.shape[0], DILATION_STEP, HD), axis=2).reshape(-1)
    return (log_norm, row_delta)


def head_grads(query, key, value, grad, usable, start_shift, log_norm, row_delta, scaling):
    seq_rows = query.shape[0]

    def segment_grads(pieces):
        parts_out = block_grads(
            pieces[0], pieces[1], pieces[2], pieces[3], pieces[4], pieces[5], pieces[6], scaling
        )
        return tuple((dense(entry) for entry in parts_out))

    window = lax.map(
        segment_grads,
        (
            by_segment(query),
            by_segment(key),
            by_segment(value),
            by_segment(grad),
            by_segment(usable),
            by_segment(log_norm),
            by_segment(row_delta),
        ),
    )
    dilated = block_grads(
        pick_rows(query, start_shift),
        pick_rows(key, start_shift),
        pick_rows(value, start_shift),
        pick_rows(grad, start_shift),
        pick_rows(usable, start_shift),
        pick_rows(log_norm, start_shift),
        pick_rows(row_delta, start_shift),
        scaling,
    )
    return tuple(
        (
            first.reshape(seq_rows // DILATION_STEP, -1) + place_cols(second, start_shift)
            for first, second in zip(window, dilated)
        )
    )


def columns(input_matrix, local_head):
    return input_matrix[:, local_head * HD : (local_head + 1) * HD]


def join_heads(dense_list, seq_rows):
    pieces = [entry.reshape(seq_rows, HD) for entry in dense_list]
    if len(pieces) == 1:
        return pieces[0].astype(jnp.bfloat16)
    return jnp.concatenate(pieces, axis=1).astype(jnp.bfloat16)


def on_device(queries, keys, values, out_grad, tissue, valid_count):
    tissue_flags = lax.all_gather(tissue, "seq", axis=0, tiled=True)
    head_queries, head_keys, head_values, head_grad = (
        lax.all_to_all(queries, "seq", split_axis=1, concat_axis=0, tiled=True),
        lax.all_to_all(keys, "seq", split_axis=1, concat_axis=0, tiled=True),
        lax.all_to_all(values, "seq", split_axis=1, concat_axis=0, tiled=True),
        lax.all_to_all(out_grad, "seq", split_axis=1, concat_axis=0, tiled=True),
    )
    seq_rows = head_queries.shape[0]
    heads_here = head_queries.shape[1] // HD
    block_rows = seq_rows // tissue_flags.shape[0]
    row_index = jnp.arange(seq_rows, dtype=jnp.int32)
    tissue_rows = jnp.broadcast_to(
        tissue_flags[:, None] == 1, (tissue_flags.shape[0], block_rows)
    ).reshape(seq_rows)
    usable = (row_index < valid_count[0]) & tissue_rows
    scaling = 1.0 / math.sqrt(HD)
    leading_head = lax.axis_index("seq") * heads_here
    start_shifts = [(leading_head + local_head) % DILATION_STEP for local_head in range(heads_here)]
    statistics = [
        head_stats(
            columns(head_queries, local_head),
            columns(head_keys, local_head),
            columns(head_values, local_head),
            usable,
            start_shifts[local_head],
            scaling,
        )
        for local_head in range(heads_here)
    ]
    normalized = [
        normalizer(statistics[local_head], columns(head_grad, local_head), usable)
        for local_head in range(heads_here)
    ]

    def grads_of(local_head):
        return head_grads(
            columns(head_queries, local_head),
            columns(head_keys, local_head),
            columns(head_values, local_head),
            columns(head_grad, local_head),
            usable,
            start_shifts[local_head],
            normalized[local_head][0],
            normalized[local_head][1],
            scaling,
        )

    results = [grads_of(local_head) for local_head in range(heads_here)]
    value_part = join_heads([entry[0] for entry in results], seq_rows)
    query_part = join_heads([entry[1] for entry in results], seq_rows)
    key_part = join_heads([entry[2] for entry in results], seq_rows)
    grad_query, grad_key, grad_value = (
        lax.all_to_all(query_part, "seq", split_axis=0, concat_axis=1, tiled=True),
        lax.all_to_all(key_part, "seq", split_axis=0, concat_axis=1, tiled=True),
        lax.all_to_all(value_part, "seq", split_axis=0, concat_axis=1, tiled=True),
    )
    return (grad_query, grad_key, grad_value)


PAIR = 2 * HD
QB = 256
FLOOR = -1e29
PEER_ORDER = (1, 6, 7, 2, 3, 4, 5)
LAST_ORDER = ((0, 0), (0, 1), (1, 0), (2, 0), (1, 1), (2, 1))
ONCE = 8


def log2_pieces():
    left, pieces = math.log(2.0), []
    for _ in range(3):
        piece = float(np.asarray(left, jnp.bfloat16))
        pieces.append(piece)
        left -= piece
    return pieces


def partner(me, step):
    other = me
    for bit in (1, 2, 4):
        other = other + bit * (1 - 2 * ((me // bit) % 2)) * ((step // bit) % 2)
    return other


def nt_dot(a, b):
    return lax.dot_general(a, b, (((1,), (1,)), ((), ())), preferred_element_type=jnp.float32)


def fused_kernel(
    n,
    q_ref,
    k_ref,
    v_ref,
    g_ref,
    tissue_ref,
    count_ref,
    grads_ref,
    buf,
    flags,
    key_side,
    query_side,
    key_cols,
    sums,
    res,
    arrive,
    once,
    tissue_here,
    staged,
):
    me = lax.axis_index("seq")
    local = q_ref.shape[0]
    rows = n * local
    pairs = buf.shape[0]
    width = pairs * PAIR
    chip = QB // local
    scaling = 1.0 / math.sqrt(HD)
    peers = [partner(me, step) for step in range(n)]

    def rows_of(device):
        return pl.ds(pl.multiple_of(device * local, local), local)

    def cols_of(device, pair):
        return pl.ds(pl.multiple_of(device * width + pair * PAIR, PAIR), PAIR)

    def remote(src, dst, send, recv, device):
        return pltpu.make_async_remote_copy(
            src_ref=src,
            dst_ref=dst,
            send_sem=send,
            recv_sem=recv,
            device_id={"seq": device},
            device_id_type=pl.DeviceIdType.MESH,
        )

    barrier = pltpu.get_barrier_semaphore()
    for step in range(1, n):
        pl.semaphore_signal(
            barrier, inc=1, device_id={"seq": peers[step]}, device_id_type=pl.DeviceIdType.MESH
        )

    flag_send, flag_recv, in_send, out_send, out_recv, own_in, own_out, small = (
        once.at[index] for index in range(ONCE)
    )
    for which in range(2):
        pltpu.make_async_copy((k_ref, v_ref)[which], staged.at[which], once.at[7]).start()
    pl.semaphore_wait(barrier, n - 1)
    pltpu.make_async_copy(staged, staged, once.at[7]).wait()

    ins = (k_ref, v_ref, q_ref, g_ref)

    def send_in(pair, group):
        for step in PEER_ORDER:
            for which in range(2 * group, 2 * group + 2):
                remote(
                    (staged.at[which] if group == 0 and pair == 0 else ins[which]).at[
                        :, cols_of(peers[step], pair)
                    ],
                    buf.at[pair, which, rows_of(me), :],
                    in_send,
                    arrive.at[pair, 1 + step // chip if group else 0],
                    peers[step],
                ).start()

    send_in(0, 0)
    tissue_copy = pltpu.make_async_copy(tissue_ref, tissue_here, small)
    tissue_copy.start()
    for pair in range(pairs):
        for which in range(4):
            pltpu.make_async_copy(
                ins[which].at[:, cols_of(me, pair)], buf.at[pair, which, rows_of(me), :], own_in
            ).start()
    tissue_copy.wait()
    spot = lax.broadcasted_iota(jnp.int32, flags.shape[1:], 1)
    blocks_here = tissue_here.shape[0]
    tissue = jnp.zeros_like(spot)
    for block in range(blocks_here):
        tissue = jnp.where(spot // (local // blocks_here) == block, tissue_here[block], tissue)
    usable = (me * local + spot < count_ref[0]) & (tissue == 1)
    flags[me] = usable.astype(jnp.float32)
    for step in PEER_ORDER:
        remote(
            flags.at[me, pl.ds(0, 1)], flags.at[me, pl.ds(0, 1)], flag_send, flag_recv, peers[step]
        ).start()
    send_in(0, 1)
    for pair in range(1, pairs):
        send_in(pair, 0)
        send_in(pair, 1)

    def landed(ref, sem):
        remote(ref, ref, in_send, sem, peers[1]).wait_recv()

    def left(ref, sem):
        remote(ref, ref, sem, out_recv, peers[1]).wait_send()

    theirs = pl.ds(0, rows - local)
    mine = buf.at[:, :, pl.ds(0, local), :]
    pltpu.make_async_copy(mine, mine, own_in).wait()
    landed(flags.at[0, pl.ds(0, n - 1)], flag_recv)
    lane = lax.broadcasted_iota(jnp.int32, (local, PAIR), 1)
    residue = lax.broadcasted_iota(jnp.int32, (local, PAIR), 0) % DILATION_STEP
    pieces = log2_pieces()
    piece = jnp.where(lane < 8, pieces[0], jnp.where(lane < 16, pieces[1], pieces[2]))
    same = (lane < 24) & (lane % DILATION_STEP == residue)
    for block in range(n):
        flag = jnp.transpose(jnp.broadcast_to(flags[block, 0:1, :], (local, PAIR)))
        off = (1.0 - flag) * NEG
        side = jnp.where(lane == 24, off, jnp.where(lane == 25, 1.0, jnp.where(same, piece, 0.0)))
        here = pl.ds(block * local, local)
        for pair in range(pairs):
            key_side[pair, here, PAIR:] = side.astype(jnp.bfloat16)
        for head in range(2 * pairs):
            shift = (me * 2 * pairs + head) % DILATION_STEP
            chosen = same & (lane % DILATION_STEP == shift)
            side = jnp.where(
                lane == 24, 1.0, jnp.where(lane == 25, off, jnp.where(chosen, 1.0, 0.0))
            )
            query_side[head, here, :] = side.astype(jnp.bfloat16)

    half = lax.broadcasted_iota(jnp.int32, (QB, PAIR), 1) // HD

    def send_out(pair, which, device):
        remote(
            res.at[pair, which, rows_of(device), :],
            grads_ref.at[which, :, cols_of(me, pair)],
            out_send,
            out_recv,
            device,
        ).start()

    for pair in range(pairs):
        landed(buf.at[pair, pl.ds(0, 2), theirs, :], arrive.at[pair, 0])
        key_side[pair, :, :PAIR] = buf[pair, 0]
        key_cols[...] = jnp.transpose(buf[pair, 0].astype(jnp.float32)).astype(jnp.bfloat16)
        sums[...] = jnp.zeros_like(sums)

        def query_block(index, carry, pair=pair):
            far = (n // chip - index) % (n // chip) if pair == 0 else n // chip - 1 - index
            for count, here in ((chip - 1, far == 0), (chip, far > 0)):

                @pl.when(here)
                def _(count=count):
                    these = pl.ds(0, count * local)
                    landed(buf.at[pair, pl.ds(2, 2), these, :], arrive.at[pair, 1 + far])

            first = partner(me - me % chip, far * chip)
            here = pl.ds(pl.multiple_of(first * local, QB), QB)
            query = buf[pair, 2, here, :].astype(jnp.float32) * scaling
            grad = buf[pair, 3, here, :].astype(jnp.float32)
            columns_out = []
            for side in range(2):
                query_h = jnp.where(half == side, query, 0.0).astype(jnp.bfloat16)
                grad_h = jnp.where(half == side, grad, 0.0).astype(jnp.bfloat16)
                extended = jnp.concatenate(
                    [query_h, query_side[2 * pair + side, here, :]], axis=1
                )
                score = nt_dot(key_side[pair], extended)
                grad_prob = nt_dot(buf[pair, 1], grad_h)
                top = jnp.maximum(jnp.max(score, axis=0, keepdims=True), FLOOR)
                weight = jnp.exp(score - top)
                total = jnp.maximum(jnp.sum(weight, axis=0, keepdims=True), 1.0)
                inverse = 1.0 / total
                delta = jnp.sum(weight * grad_prob, axis=0, keepdims=True) * inverse
                prob = weight * inverse
                dscore = (prob * (grad_prob - delta)).astype(jnp.bfloat16)
                sums[0] += jnp.dot(dscore, query_h, preferred_element_type=jnp.float32)
                sums[1] += jnp.dot(
                    prob.astype(jnp.bfloat16), grad_h, preferred_element_type=jnp.float32
                )
                columns_out.append(
                    jnp.dot(
                        key_cols[side * HD : (side + 1) * HD, :],
                        dscore,
                        preferred_element_type=jnp.float32,
                    )
                )
            grad_query = jnp.transpose(jnp.concatenate(columns_out, axis=0)) * scaling
            res[pair, 0, here, :] = grad_query.astype(jnp.bfloat16)
            for part in range(chip):
                step = far * chip + part

                def leaves(step=step):
                    send_out(pair, 0, partner(me, step))

                if part == 0:
                    pl.when(step > 0)(leaves)
                else:
                    leaves()
            return carry

        lax.fori_loop(0, rows // QB, query_block, 0)
        res[pair, 1] = sums[0].astype(jnp.bfloat16)
        res[pair, 2] = sums[1].astype(jnp.bfloat16)
        send_out(pair, pl.ds(1, 2), peers[1])
        here_chip = me // 2
        first = here_chip + 3 * ((3 - here_chip) // 3)
        second = 3 - 2 * (first // 3)
        order = (first, second, 6 - first - second)
        for place, core in LAST_ORDER:
            step = 2 * order[place] + core + (me % 2) * (1 - 2 * core)
            send_out(pair, pl.ds(1, 2), partner(me, step))
        pltpu.make_async_copy(
            res.at[pair, :, rows_of(me), :], grads_ref.at[:, :, cols_of(me, pair)], own_out
        ).start()
    left(flags.at[0, pl.ds(0, n - 1)], flag_send)
    left(buf.at[:, :, theirs, :], in_send)
    mine = res.at[:, :, pl.ds(0, local), :]
    pltpu.make_async_copy(mine, mine, own_out).wait()
    left(res.at[:, :, theirs, :], out_send)
    landed(res.at[:, :, theirs, :], out_recv)


def write_kernel(grads_ref, dq_ref, dk_ref, dv_ref, sem):
    copies = [
        pltpu.make_async_copy(grads_ref.at[which], out, sem.at[0])
        for which, out in enumerate((dq_ref, dk_ref, dv_ref))
    ]
    for copy in copies:
        copy.start()
    for copy in copies:
        copy.wait()


def on_device_fused(n, queries, keys, values, out_grad, tissue, valid_count):
    local, features = queries.shape
    rows = n * local
    pairs = features // n // PAIR
    hbm = pl.BlockSpec(memory_space=pltpu.HBM)
    vmem = pl.BlockSpec(memory_space=pltpu.VMEM)
    smem = pl.BlockSpec(memory_space=pltpu.SMEM)
    dma = pltpu.SemaphoreType.DMA
    grads = pl.pallas_call(
        functools.partial(fused_kernel, n),
        out_shape=pltpu.VMEM((3, local, features), jnp.bfloat16),
        in_specs=[hbm] * 5 + [smem],
        out_specs=vmem,
        scratch_shapes=[
            pltpu.VMEM((pairs, 4, rows, PAIR), jnp.bfloat16),
            pltpu.VMEM((n, 8, local), jnp.float32),
            pltpu.VMEM((pairs, rows, 2 * PAIR), jnp.bfloat16),
            pltpu.VMEM((2 * pairs, rows, PAIR), jnp.bfloat16),
            pltpu.VMEM((PAIR, rows), jnp.bfloat16),
            pltpu.VMEM((2, rows, PAIR), jnp.float32),
            pltpu.VMEM((pairs, 3, rows, PAIR), jnp.bfloat16),
            dma((pairs, 1 + rows // QB)),
            dma((ONCE,)),
            pltpu.SMEM(tissue.shape, jnp.int32),
            pltpu.VMEM((2, local, features), jnp.bfloat16),
        ],
        compiler_params=pltpu.CompilerParams(
            collective_id=0, has_side_effects=True, vmem_limit_bytes=48 * 2**20
        ),
        name="attention_backward",
    )(
        *(
            pltpu.with_memory_space_constraint(entry, pltpu.HBM)
            for entry in (queries, keys, values, out_grad, tissue)
        ),
        valid_count,
    )
    return tuple(
        pl.pallas_call(
            write_kernel,
            out_shape=[jax.ShapeDtypeStruct((local, features), jnp.bfloat16)] * 3,
            in_specs=[vmem],
            out_specs=[hbm] * 3,
            scratch_shapes=[dma((1,))],
            compiler_params=pltpu.CompilerParams(vmem_limit_bytes=4 * 2**20),
            name="write_gradients",
        )(grads)
    )


def solution(mesh):
    in_specs = (
        P(("slide", "seq"), None),
        P(("slide", "seq"), None),
        P(("slide", "seq"), None),
        P(("slide", "seq"), None),
        P(("slide", "seq")),
        P("slide"),
    )
    out_specs = (P(("slide", "seq"), None), P(("slide", "seq"), None), P(("slide", "seq"), None))
    n = mesh.shape["seq"]

    def body(queries, keys, values, out_grad, tissue, valid_count):
        arguments = (queries, keys, values, out_grad, tissue, valid_count)
        local, features = queries.shape
        if n == 8 and local == PAIR and n * local == SEG and features % (n * PAIR) == 0:
            return on_device_fused(n, *arguments)
        return on_device(*arguments)

    return jax.shard_map(
        body, mesh=mesh, in_specs=in_specs, out_specs=out_specs, check_vma=False
    )
```

```python
import functools
import math

import jax
import jax.numpy as jnp
import numpy as np
from jax import lax
from jax.experimental import pallas as pl
from jax.experimental.pallas import tpu as pltpu
from jax.sharding import PartitionSpec as P

HD = 64
SEG = 1024
DILATION_STEP = 8


NEG = -1e30


def dense(input_matrix):
    return input_matrix.reshape(
        input_matrix.shape[0] // DILATION_STEP, DILATION_STEP * input_matrix.shape[1]
    )


def block_stats(query_rows, key_rows, value_rows, usable, scaling):
    scores = (
        jnp.einsum("qd,kd->qk", query_rows, key_rows, preferred_element_type=jnp.float32) * scaling
    )
    allowed = usable[:, None] & usable[None, :]
    row_max = jnp.max(jnp.where(allowed, scores, NEG), axis=1)
    weights = jnp.where(allowed, jnp.exp(scores - row_max[:, None]), 0.0)
    totals = jnp.sum(weights, axis=1)
    summed = jnp.einsum(
        "qk,kd->qd", weights.astype(jnp.bfloat16), value_rows, preferred_element_type=jnp.float32
    )
    return (row_max, totals, summed)


def block_grads(query_rows, key_rows, value_rows, grad_rows, usable, log_norm, row_delta, scaling):
    scores = (
        jnp.einsum("qd,kd->qk", query_rows, key_rows, preferred_element_type=jnp.float32) * scaling
    )
    allowed = usable[:, None] & usable[None, :]
    probs = jnp.where(allowed, jnp.exp(scores - log_norm[:, None]), 0.0)
    results = ()
    results = results + (
        jnp.einsum(
            "qk,qd->kd", probs.astype(jnp.bfloat16), grad_rows, preferred_element_type=jnp.float32
        ),
    )
    grad_probs = jnp.einsum("qd,kd->qk", grad_rows, value_rows, preferred_element_type=jnp.float32)
    grad_scores = (probs * (grad_probs - row_delta[:, None])).astype(jnp.bfloat16)
    grad_query = (
        jnp.einsum("qk,kd->qd", grad_scores, key_rows, preferred_element_type=jnp.float32) * scaling
    )
    grad_key = (
        jnp.einsum("qk,qd->kd", grad_scores, query_rows, preferred_element_type=jnp.float32)
        * scaling
    )
    results = results + (grad_query, grad_key)
    return results


def pick_rows(input_matrix, start_shift):
    if input_matrix.ndim == 1:
        reshaped_tensor = input_matrix.reshape(
            input_matrix.shape[0] // DILATION_STEP, DILATION_STEP
        )
        return lax.dynamic_index_in_dim(reshaped_tensor, start_shift, axis=1, keepdims=False)
    width = input_matrix.shape[1]
    return lax.dynamic_slice_in_dim(dense(input_matrix), start_shift * width, width, 1)


def spread_rows(input_matrix, start_shift, filler):
    picked_index = jnp.arange(DILATION_STEP, dtype=jnp.int32) == start_shift
    return jnp.where(picked_index[None, :], input_matrix[:, None], filler).reshape(-1)


def place_cols(input_matrix, start_shift):
    width = input_matrix.shape[1]
    picked_block = jnp.arange(DILATION_STEP * width, dtype=jnp.int32) // width == start_shift
    return jnp.where(picked_block[None, :], jnp.tile(input_matrix, (1, DILATION_STEP)), 0.0)


def by_segment(input_matrix):
    return input_matrix.reshape((input_matrix.shape[0] // SEG, SEG) + input_matrix.shape[1:])


def head_stats(query, key, value, usable, start_shift, scaling):
    seq_rows = query.shape[0]

    def segment_stats(pieces):
        row_max, totals, summed = block_stats(pieces[0], pieces[1], pieces[2], pieces[3], scaling)
        return (row_max, totals, dense(summed))

    max_w, sum_w, acc_w = lax.map(
        segment_stats, (by_segment(query), by_segment(key), by_segment(value), by_segment(usable))
    )
    usable_d = pick_rows(usable, start_shift)
    max_d, sum_d, acc_d = block_stats(
        pick_rows(query, start_shift),
        pick_rows(key, start_shift),
        pick_rows(value, start_shift),
        usable_d,
        scaling,
    )
    return (
        max_w.reshape(seq_rows),
        sum_w.reshape(seq_rows),
        acc_w.reshape(seq_rows // DILATION_STEP, -1),
        spread_rows(max_d, start_shift, NEG),
        spread_rows(sum_d, start_shift, 0.0),
        place_cols(acc_d, start_shift),
    )


def normalizer(statistics, grad, usable):
    max_w, sum_w, acc_w, max_d, sum_d, acc_d = statistics
    largest = jnp.maximum(max_w, max_d)
    totals = sum_w * jnp.exp(max_w - largest) + sum_d * jnp.exp(max_d - largest)
    log_norm = jnp.where(usable, largest + jnp.log(jnp.where(usable, totals, 1.0)), 0.0)
    weight_window = jnp.repeat(jnp.exp(max_w - log_norm).reshape(-1, DILATION_STEP), HD, axis=1)
    weight_dilated = jnp.repeat(jnp.exp(max_d - log_norm).reshape(-1, DILATION_STEP), HD, axis=1)
    attended = weight_window * acc_w + weight_dilated * acc_d
    products = dense(grad).astype(jnp.float32) * attended
    row_delta = jnp.sum(products.reshape(products.shape[0], DILATION_STEP, HD), axis=2).reshape(-1)
    return (log_norm, row_delta)


def head_grads(query, key, value, grad, usable, start_shift, log_norm, row_delta, scaling):
    seq_rows = query.shape[0]

    def segment_grads(pieces):
        parts_out = block_grads(
            pieces[0], pieces[1], pieces[2], pieces[3], pieces[4], pieces[5], pieces[6], scaling
        )
        return tuple((dense(entry) for entry in parts_out))

    window = lax.map(
        segment_grads,
        (
            by_segment(query),
            by_segment(key),
            by_segment(value),
            by_segment(grad),
            by_segment(usable),
            by_segment(log_norm),
            by_segment(row_delta),
        ),
    )
    dilated = block_grads(
        pick_rows(query, start_shift),
        pick_rows(key, start_shift),
        pick_rows(value, start_shift),
        pick_rows(grad, start_shift),
        pick_rows(usable, start_shift),
        pick_rows(log_norm, start_shift),
        pick_rows(row_delta, start_shift),
        scaling,
    )
    return tuple(
        (
            first.reshape(seq_rows // DILATION_STEP, -1) + place_cols(second, start_shift)
            for first, second in zip(window, dilated)
        )
    )


def columns(input_matrix, local_head):
    return input_matrix[:, local_head * HD : (local_head + 1) * HD]


def join_heads(dense_list, seq_rows):
    pieces = [entry.reshape(seq_rows, HD) for entry in dense_list]
    if len(pieces) == 1:
        return pieces[0].astype(jnp.bfloat16)
    return jnp.concatenate(pieces, axis=1).astype(jnp.bfloat16)


def on_device(queries, keys, values, out_grad, tissue, valid_count):
    tissue_flags = lax.all_gather(tissue, "seq", axis=0, tiled=True)
    head_queries, head_keys, head_values, head_grad = (
        lax.all_to_all(queries, "seq", split_axis=1, concat_axis=0, tiled=True),
        lax.all_to_all(keys, "seq", split_axis=1, concat_axis=0, tiled=True),
        lax.all_to_all(values, "seq", split_axis=1, concat_axis=0, tiled=True),
        lax.all_to_all(out_grad, "seq", split_axis=1, concat_axis=0, tiled=True),
    )
    seq_rows = head_queries.shape[0]
    heads_here = head_queries.shape[1] // HD
    block_rows = seq_rows // tissue_flags.shape[0]
    row_index = jnp.arange(seq_rows, dtype=jnp.int32)
    tissue_rows = jnp.broadcast_to(
        tissue_flags[:, None] == 1, (tissue_flags.shape[0], block_rows)
    ).reshape(seq_rows)
    usable = (row_index < valid_count[0]) & tissue_rows
    scaling = 1.0 / math.sqrt(HD)
    leading_head = lax.axis_index("seq") * heads_here
    start_shifts = [(leading_head + local_head) % DILATION_STEP for local_head in range(heads_here)]
    statistics = [
        head_stats(
            columns(head_queries, local_head),
            columns(head_keys, local_head),
            columns(head_values, local_head),
            usable,
            start_shifts[local_head],
            scaling,
        )
        for local_head in range(heads_here)
    ]
    normalized = [
        normalizer(statistics[local_head], columns(head_grad, local_head), usable)
        for local_head in range(heads_here)
    ]

    def grads_of(local_head):
        return head_grads(
            columns(head_queries, local_head),
            columns(head_keys, local_head),
            columns(head_values, local_head),
            columns(head_grad, local_head),
            usable,
            start_shifts[local_head],
            normalized[local_head][0],
            normalized[local_head][1],
            scaling,
        )

    results = [grads_of(local_head) for local_head in range(heads_here)]
    value_part = join_heads([entry[0] for entry in results], seq_rows)
    query_part = join_heads([entry[1] for entry in results], seq_rows)
    key_part = join_heads([entry[2] for entry in results], seq_rows)
    grad_query, grad_key, grad_value = (
        lax.all_to_all(query_part, "seq", split_axis=0, concat_axis=1, tiled=True),
        lax.all_to_all(key_part, "seq", split_axis=0, concat_axis=1, tiled=True),
        lax.all_to_all(value_part, "seq", split_axis=0, concat_axis=1, tiled=True),
    )
    return (grad_query, grad_key, grad_value)


PAIR = 2 * HD
QB = 256
FLOOR = -1e29
PEER_ORDER = (1, 6, 7, 2, 3, 4, 5)
LAST_ORDER = ((0, 0), (0, 1), (1, 0), (2, 0), (1, 1), (2, 1))
ONCE = 8


def log2_pieces():
    left, pieces = math.log(2.0), []
    for _ in range(3):
        piece = float(np.asarray(left, jnp.bfloat16))
        pieces.append(piece)
        left -= piece
    return pieces


def partner(me, step):
    other = me
    for bit in (1, 2, 4):
        other = other + bit * (1 - 2 * ((me // bit) % 2)) * ((step // bit) % 2)
    return other


def nt_dot(a, b):
    return lax.dot_general(a, b, (((1,), (1,)), ((), ())), preferred_element_type=jnp.float32)


def fused_kernel(
    n,
    q_ref,
    k_ref,
    v_ref,
    g_ref,
    tissue_ref,
    count_ref,
    grads_ref,
    buf,
    flags,
    key_side,
    query_side,
    key_cols,
    sums,
    res,
    arrive,
    once,
    tissue_here,
    staged,
):
    me = lax.axis_index("seq")
    local = q_ref.shape[0]
    rows = n * local
    pairs = buf.shape[0]
    width = pairs * PAIR
    chip = QB // local
    scaling = 1.0 / math.sqrt(HD)
    peers = [partner(me, step) for step in range(n)]

    def rows_of(device):
        return pl.ds(pl.multiple_of(device * local, local), local)

    def cols_of(device, pair):
        return pl.ds(pl.multiple_of(device * width + pair * PAIR, PAIR), PAIR)

    def remote(src, dst, send, recv, device):
        return pltpu.make_async_remote_copy(
            src_ref=src,
            dst_ref=dst,
            send_sem=send,
            recv_sem=recv,
            device_id={"seq": device},
            device_id_type=pl.DeviceIdType.MESH,
        )

    barrier = pltpu.get_barrier_semaphore()
    for step in range(1, n):
        pl.semaphore_signal(
            barrier, inc=1, device_id={"seq": peers[step]}, device_id_type=pl.DeviceIdType.MESH
        )

    flag_send, flag_recv, in_send, out_send, out_recv, own_in, own_out, small = (
        once.at[index] for index in range(ONCE)
    )
    for which in range(2):
        for device in range(n):
            pltpu.make_async_copy(
                (k_ref, v_ref)[which].at[:, pl.ds(device * width, PAIR)],
                staged.at[which, :, pl.ds(device * PAIR, PAIR)],
                once.at[7],
            ).start()
    pl.semaphore_wait(barrier, n - 1)
    pltpu.make_async_copy(staged, staged, once.at[7]).wait()

    ins = (k_ref, v_ref, q_ref, g_ref)

    def send_in(pair, group):
        for step in PEER_ORDER:
            for which in range(2 * group, 2 * group + 2):
                remote(
                    staged.at[which, :, pl.ds(pl.multiple_of(peers[step] * PAIR, PAIR), PAIR)]
                    if group == 0 and pair == 0
                    else ins[which].at[:, cols_of(peers[step], pair)],
                    buf.at[pair, which, rows_of(me), :],
                    in_send,
                    arrive.at[pair, 1 + step // chip if group else 0],
                    peers[step],
                ).start()

    send_in(0, 0)
    tissue_copy = pltpu.make_async_copy(tissue_ref, tissue_here, small)
    tissue_copy.start()
    for pair in range(pairs):
        for which in range(4):
            pltpu.make_async_copy(
                ins[which].at[:, cols_of(me, pair)], buf.at[pair, which, rows_of(me), :], own_in
            ).start()
    tissue_copy.wait()
    spot = lax.broadcasted_iota(jnp.int32, flags.shape[1:], 1)
    blocks_here = tissue_here.shape[0]
    tissue = jnp.zeros_like(spot)
    for block in range(blocks_here):
        tissue = jnp.where(spot // (local // blocks_here) == block, tissue_here[block], tissue)
    usable = (me * local + spot < count_ref[0]) & (tissue == 1)
    flags[me] = usable.astype(jnp.float32)
    for step in PEER_ORDER:
        remote(
            flags.at[me, pl.ds(0, 1)], flags.at[me, pl.ds(0, 1)], flag_send, flag_recv, peers[step]
        ).start()
    send_in(0, 1)
    for pair in range(1, pairs):
        send_in(pair, 0)
        send_in(pair, 1)

    def landed(ref, sem):
        remote(ref, ref, in_send, sem, peers[1]).wait_recv()

    def left(ref, sem):
        remote(ref, ref, sem, out_recv, peers[1]).wait_send()

    theirs = pl.ds(0, rows - local)
    mine = buf.at[:, :, pl.ds(0, local), :]
    pltpu.make_async_copy(mine, mine, own_in).wait()
    landed(flags.at[0, pl.ds(0, n - 1)], flag_recv)
    lane = lax.broadcasted_iota(jnp.int32, (local, PAIR), 1)
    residue = lax.broadcasted_iota(jnp.int32, (local, PAIR), 0) % DILATION_STEP
    pieces = log2_pieces()
    piece = jnp.where(lane < 8, pieces[0], jnp.where(lane < 16, pieces[1], pieces[2]))
    same = (lane < 24) & (lane % DILATION_STEP == residue)
    for block in range(n):
        flag = jnp.transpose(jnp.broadcast_to(flags[block, 0:1, :], (local, PAIR)))
        off = (1.0 - flag) * NEG
        side = jnp.where(lane == 24, off, jnp.where(lane == 25, 1.0, jnp.where(same, piece, 0.0)))
        here = pl.ds(block * local, local)
        for pair in range(pairs):
            key_side[pair, here, PAIR:] = side.astype(jnp.bfloat16)
        for head in range(2 * pairs):
            shift = (me * 2 * pairs + head) % DILATION_STEP
            chosen = same & (lane % DILATION_STEP == shift)
            side = jnp.where(
                lane == 24, 1.0, jnp.where(lane == 25, off, jnp.where(chosen, 1.0, 0.0))
            )
            query_side[head, here, :] = side.astype(jnp.bfloat16)

    half = lax.broadcasted_iota(jnp.int32, (QB, PAIR), 1) // HD

    def send_out(pair, which, device):
        remote(
            res.at[pair, which, rows_of(device), :],
            grads_ref.at[which, :, cols_of(me, pair)],
            out_send,
            out_recv,
            device,
        ).start()

    for pair in range(pairs):
        landed(buf.at[pair, pl.ds(0, 2), theirs, :], arrive.at[pair, 0])
        key_side[pair, :, :PAIR] = buf[pair, 0]
        key_cols[...] = jnp.transpose(buf[pair, 0].astype(jnp.float32)).astype(jnp.bfloat16)
        sums[...] = jnp.zeros_like(sums)

        def query_block(index, carry, pair=pair):
            far = (n // chip - index) % (n // chip) if pair == 0 else n // chip - 1 - index
            for count, here in ((chip - 1, far == 0), (chip, far > 0)):

                @pl.when(here)
                def _(count=count):
                    these = pl.ds(0, count * local)
                    landed(buf.at[pair, pl.ds(2, 2), these, :], arrive.at[pair, 1 + far])

            first = partner(me - me % chip, far * chip)
            here = pl.ds(pl.multiple_of(first * local, QB), QB)
            query = buf[pair, 2, here, :].astype(jnp.float32) * scaling
            grad = buf[pair, 3, here, :].astype(jnp.float32)
            columns_out = []
            for side in range(2):
                query_h = jnp.where(half == side, query, 0.0).astype(jnp.bfloat16)
                grad_h = jnp.where(half == side, grad, 0.0).astype(jnp.bfloat16)
                extended = jnp.concatenate(
                    [query_h, query_side[2 * pair + side, here, :]], axis=1
                )
                score = nt_dot(key_side[pair], extended)
                grad_prob = nt_dot(buf[pair, 1], grad_h)
                top = jnp.maximum(jnp.max(score, axis=0, keepdims=True), FLOOR)
                weight = jnp.exp(score - top)
                total = jnp.maximum(jnp.sum(weight, axis=0, keepdims=True), 1.0)
                inverse = 1.0 / total
                delta = jnp.sum(weight * grad_prob, axis=0, keepdims=True) * inverse
                prob = weight * inverse
                dscore = (prob * (grad_prob - delta)).astype(jnp.bfloat16)
                sums[0] += jnp.dot(dscore, query_h, preferred_element_type=jnp.float32)
                sums[1] += jnp.dot(
                    prob.astype(jnp.bfloat16), grad_h, preferred_element_type=jnp.float32
                )
                columns_out.append(
                    jnp.dot(
                        key_cols[side * HD : (side + 1) * HD, :],
                        dscore,
                        preferred_element_type=jnp.float32,
                    )
                )
            grad_query = jnp.transpose(jnp.concatenate(columns_out, axis=0)) * scaling
            res[pair, 0, here, :] = grad_query.astype(jnp.bfloat16)
            for part in range(chip):
                step = far * chip + part

                def leaves(step=step):
                    send_out(pair, 0, partner(me, step))

                if part == 0:
                    pl.when(step > 0)(leaves)
                else:
                    leaves()
            return carry

        lax.fori_loop(0, rows // QB, query_block, 0)
        res[pair, 1] = sums[0].astype(jnp.bfloat16)
        res[pair, 2] = sums[1].astype(jnp.bfloat16)
        send_out(pair, pl.ds(1, 2), peers[1])
        here_chip = me // 2
        first = here_chip + 3 * ((3 - here_chip) // 3)
        second = 3 - 2 * (first // 3)
        order = (first, second, 6 - first - second)
        for place, core in LAST_ORDER:
            step = 2 * order[place] + core + (me % 2) * (1 - 2 * core)
            send_out(pair, pl.ds(1, 2), partner(me, step))
        pltpu.make_async_copy(
            res.at[pair, :, rows_of(me), :], grads_ref.at[:, :, cols_of(me, pair)], own_out
        ).start()
    left(flags.at[0, pl.ds(0, n - 1)], flag_send)
    left(buf.at[:, :, theirs, :], in_send)
    mine = res.at[:, :, pl.ds(0, local), :]
    pltpu.make_async_copy(mine, mine, own_out).wait()
    left(res.at[:, :, theirs, :], out_send)
    landed(res.at[:, :, theirs, :], out_recv)


def write_kernel(grads_ref, dq_ref, dk_ref, dv_ref, sem):
    copies = [
        pltpu.make_async_copy(grads_ref.at[which], out, sem.at[0])
        for which, out in enumerate((dq_ref, dk_ref, dv_ref))
    ]
    for copy in copies:
        copy.start()
    for copy in copies:
        copy.wait()


def on_device_fused(n, queries, keys, values, out_grad, tissue, valid_count):
    local, features = queries.shape
    rows = n * local
    pairs = features // n // PAIR
    hbm = pl.BlockSpec(memory_space=pltpu.HBM)
    vmem = pl.BlockSpec(memory_space=pltpu.VMEM)
    smem = pl.BlockSpec(memory_space=pltpu.SMEM)
    dma = pltpu.SemaphoreType.DMA
    grads = pl.pallas_call(
        functools.partial(fused_kernel, n),
        out_shape=pltpu.VMEM((3, local, features), jnp.bfloat16),
        in_specs=[hbm] * 5 + [smem],
        out_specs=vmem,
        scratch_shapes=[
            pltpu.VMEM((pairs, 4, rows, PAIR), jnp.bfloat16),
            pltpu.VMEM((n, 8, local), jnp.float32),
            pltpu.VMEM((pairs, rows, 2 * PAIR), jnp.bfloat16),
            pltpu.VMEM((2 * pairs, rows, PAIR), jnp.bfloat16),
            pltpu.VMEM((PAIR, rows), jnp.bfloat16),
            pltpu.VMEM((2, rows, PAIR), jnp.float32),
            pltpu.VMEM((pairs, 3, rows, PAIR), jnp.bfloat16),
            dma((pairs, 1 + rows // QB)),
            dma((ONCE,)),
            pltpu.SMEM(tissue.shape, jnp.int32),
            pltpu.VMEM((2, local, features // pairs), jnp.bfloat16),
        ],
        compiler_params=pltpu.CompilerParams(
            collective_id=0, has_side_effects=True, vmem_limit_bytes=48 * 2**20
        ),
        name="attention_backward",
    )(
        *(
            pltpu.with_memory_space_constraint(entry, pltpu.HBM)
            for entry in (queries, keys, values, out_grad, tissue)
        ),
        valid_count,
    )
    return tuple(
        pl.pallas_call(
            write_kernel,
            out_shape=[jax.ShapeDtypeStruct((local, features), jnp.bfloat16)] * 3,
            in_specs=[vmem],
            out_specs=[hbm] * 3,
            scratch_shapes=[dma((1,))],
            compiler_params=pltpu.CompilerParams(vmem_limit_bytes=4 * 2**20),
            name="write_gradients",
        )(grads)
    )


def solution(mesh):
    in_specs = (
        P(("slide", "seq"), None),
        P(("slide", "seq"), None),
        P(("slide", "seq"), None),
        P(("slide", "seq"), None),
        P(("slide", "seq")),
        P("slide"),
    )
    out_specs = (P(("slide", "seq"), None), P(("slide", "seq"), None), P(("slide", "seq"), None))
    n = mesh.shape["seq"]

    def body(queries, keys, values, out_grad, tissue, valid_count):
        arguments = (queries, keys, values, out_grad, tissue, valid_count)
        local, features = queries.shape
        if n == 8 and local == PAIR and n * local == SEG and features % (n * PAIR) == 0:
            return on_device_fused(n, *arguments)
        return on_device(*arguments)

    return jax.shard_map(
        body, mesh=mesh, in_specs=in_specs, out_specs=out_specs, check_vma=False
    )
```

```python
import functools
import math

import jax
import jax.numpy as jnp
import numpy as np
from jax import lax
from jax.experimental import pallas as pl
from jax.experimental.pallas import tpu as pltpu
from jax.sharding import PartitionSpec as P

HD = 64
SEG = 1024
DILATION_STEP = 8


NEG = -1e30


def dense(input_matrix):
    return input_matrix.reshape(
        input_matrix.shape[0] // DILATION_STEP, DILATION_STEP * input_matrix.shape[1]
    )


def block_stats(query_rows, key_rows, value_rows, usable, scaling):
    scores = (
        jnp.einsum("qd,kd->qk", query_rows, key_rows, preferred_element_type=jnp.float32) * scaling
    )
    allowed = usable[:, None] & usable[None, :]
    row_max = jnp.max(jnp.where(allowed, scores, NEG), axis=1)
    weights = jnp.where(allowed, jnp.exp(scores - row_max[:, None]), 0.0)
    totals = jnp.sum(weights, axis=1)
    summed = jnp.einsum(
        "qk,kd->qd", weights.astype(jnp.bfloat16), value_rows, preferred_element_type=jnp.float32
    )
    return (row_max, totals, summed)


def block_grads(query_rows, key_rows, value_rows, grad_rows, usable, log_norm, row_delta, scaling):
    scores = (
        jnp.einsum("qd,kd->qk", query_rows, key_rows, preferred_element_type=jnp.float32) * scaling
    )
    allowed = usable[:, None] & usable[None, :]
    probs = jnp.where(allowed, jnp.exp(scores - log_norm[:, None]), 0.0)
    results = ()
    results = results + (
        jnp.einsum(
            "qk,qd->kd", probs.astype(jnp.bfloat16), grad_rows, preferred_element_type=jnp.float32
        ),
    )
    grad_probs = jnp.einsum("qd,kd->qk", grad_rows, value_rows, preferred_element_type=jnp.float32)
    grad_scores = (probs * (grad_probs - row_delta[:, None])).astype(jnp.bfloat16)
    grad_query = (
        jnp.einsum("qk,kd->qd", grad_scores, key_rows, preferred_element_type=jnp.float32) * scaling
    )
    grad_key = (
        jnp.einsum("qk,qd->kd", grad_scores, query_rows, preferred_element_type=jnp.float32)
        * scaling
    )
    results = results + (grad_query, grad_key)
    return results


def pick_rows(input_matrix, start_shift):
    if input_matrix.ndim == 1:
        reshaped_tensor = input_matrix.reshape(
            input_matrix.shape[0] // DILATION_STEP, DILATION_STEP
        )
        return lax.dynamic_index_in_dim(reshaped_tensor, start_shift, axis=1, keepdims=False)
    width = input_matrix.shape[1]
    return lax.dynamic_slice_in_dim(dense(input_matrix), start_shift * width, width, 1)


def spread_rows(input_matrix, start_shift, filler):
    picked_index = jnp.arange(DILATION_STEP, dtype=jnp.int32) == start_shift
    return jnp.where(picked_index[None, :], input_matrix[:, None], filler).reshape(-1)


def place_cols(input_matrix, start_shift):
    width = input_matrix.shape[1]
    picked_block = jnp.arange(DILATION_STEP * width, dtype=jnp.int32) // width == start_shift
    return jnp.where(picked_block[None, :], jnp.tile(input_matrix, (1, DILATION_STEP)), 0.0)


def by_segment(input_matrix):
    return input_matrix.reshape((input_matrix.shape[0] // SEG, SEG) + input_matrix.shape[1:])


def head_stats(query, key, value, usable, start_shift, scaling):
    seq_rows = query.shape[0]

    def segment_stats(pieces):
        row_max, totals, summed = block_stats(pieces[0], pieces[1], pieces[2], pieces[3], scaling)
        return (row_max, totals, dense(summed))

    max_w, sum_w, acc_w = lax.map(
        segment_stats, (by_segment(query), by_segment(key), by_segment(value), by_segment(usable))
    )
    usable_d = pick_rows(usable, start_shift)
    max_d, sum_d, acc_d = block_stats(
        pick_rows(query, start_shift),
        pick_rows(key, start_shift),
        pick_rows(value, start_shift),
        usable_d,
        scaling,
    )
    return (
        max_w.reshape(seq_rows),
        sum_w.reshape(seq_rows),
        acc_w.reshape(seq_rows // DILATION_STEP, -1),
        spread_rows(max_d, start_shift, NEG),
        spread_rows(sum_d, start_shift, 0.0),
        place_cols(acc_d, start_shift),
    )


def normalizer(statistics, grad, usable):
    max_w, sum_w, acc_w, max_d, sum_d, acc_d = statistics
    largest = jnp.maximum(max_w, max_d)
    totals = sum_w * jnp.exp(max_w - largest) + sum_d * jnp.exp(max_d - largest)
    log_norm = jnp.where(usable, largest + jnp.log(jnp.where(usable, totals, 1.0)), 0.0)
    weight_window = jnp.repeat(jnp.exp(max_w - log_norm).reshape(-1, DILATION_STEP), HD, axis=1)
    weight_dilated = jnp.repeat(jnp.exp(max_d - log_norm).reshape(-1, DILATION_STEP), HD, axis=1)
    attended = weight_window * acc_w + weight_dilated * acc_d
    products = dense(grad).astype(jnp.float32) * attended
    row_delta = jnp.sum(products.reshape(products.shape[0], DILATION_STEP, HD), axis=2).reshape(-1)
    return (log_norm, row_delta)


def head_grads(query, key, value, grad, usable, start_shift, log_norm, row_delta, scaling):
    seq_rows = query.shape[0]

    def segment_grads(pieces):
        parts_out = block_grads(
            pieces[0], pieces[1], pieces[2], pieces[3], pieces[4], pieces[5], pieces[6], scaling
        )
        return tuple((dense(entry) for entry in parts_out))

    window = lax.map(
        segment_grads,
        (
            by_segment(query),
            by_segment(key),
            by_segment(value),
            by_segment(grad),
            by_segment(usable),
            by_segment(log_norm),
            by_segment(row_delta),
        ),
    )
    dilated = block_grads(
        pick_rows(query, start_shift),
        pick_rows(key, start_shift),
        pick_rows(value, start_shift),
        pick_rows(grad, start_shift),
        pick_rows(usable, start_shift),
        pick_rows(log_norm, start_shift),
        pick_rows(row_delta, start_shift),
        scaling,
    )
    return tuple(
        (
            first.reshape(seq_rows // DILATION_STEP, -1) + place_cols(second, start_shift)
            for first, second in zip(window, dilated)
        )
    )


def columns(input_matrix, local_head):
    return input_matrix[:, local_head * HD : (local_head + 1) * HD]


def join_heads(dense_list, seq_rows):
    pieces = [entry.reshape(seq_rows, HD) for entry in dense_list]
    if len(pieces) == 1:
        return pieces[0].astype(jnp.bfloat16)
    return jnp.concatenate(pieces, axis=1).astype(jnp.bfloat16)


def on_device(queries, keys, values, out_grad, tissue, valid_count):
    tissue_flags = lax.all_gather(tissue, "seq", axis=0, tiled=True)
    head_queries, head_keys, head_values, head_grad = (
        lax.all_to_all(queries, "seq", split_axis=1, concat_axis=0, tiled=True),
        lax.all_to_all(keys, "seq", split_axis=1, concat_axis=0, tiled=True),
        lax.all_to_all(values, "seq", split_axis=1, concat_axis=0, tiled=True),
        lax.all_to_all(out_grad, "seq", split_axis=1, concat_axis=0, tiled=True),
    )
    seq_rows = head_queries.shape[0]
    heads_here = head_queries.shape[1] // HD
    block_rows = seq_rows // tissue_flags.shape[0]
    row_index = jnp.arange(seq_rows, dtype=jnp.int32)
    tissue_rows = jnp.broadcast_to(
        tissue_flags[:, None] == 1, (tissue_flags.shape[0], block_rows)
    ).reshape(seq_rows)
    usable = (row_index < valid_count[0]) & tissue_rows
    scaling = 1.0 / math.sqrt(HD)
    leading_head = lax.axis_index("seq") * heads_here
    start_shifts = [(leading_head + local_head) % DILATION_STEP for local_head in range(heads_here)]
    statistics = [
        head_stats(
            columns(head_queries, local_head),
            columns(head_keys, local_head),
            columns(head_values, local_head),
            usable,
            start_shifts[local_head],
            scaling,
        )
        for local_head in range(heads_here)
    ]
    normalized = [
        normalizer(statistics[local_head], columns(head_grad, local_head), usable)
        for local_head in range(heads_here)
    ]

    def grads_of(local_head):
        return head_grads(
            columns(head_queries, local_head),
            columns(head_keys, local_head),
            columns(head_values, local_head),
            columns(head_grad, local_head),
            usable,
            start_shifts[local_head],
            normalized[local_head][0],
            normalized[local_head][1],
            scaling,
        )

    results = [grads_of(local_head) for local_head in range(heads_here)]
    value_part = join_heads([entry[0] for entry in results], seq_rows)
    query_part = join_heads([entry[1] for entry in results], seq_rows)
    key_part = join_heads([entry[2] for entry in results], seq_rows)
    grad_query, grad_key, grad_value = (
        lax.all_to_all(query_part, "seq", split_axis=0, concat_axis=1, tiled=True),
        lax.all_to_all(key_part, "seq", split_axis=0, concat_axis=1, tiled=True),
        lax.all_to_all(value_part, "seq", split_axis=0, concat_axis=1, tiled=True),
    )
    return (grad_query, grad_key, grad_value)


PAIR = 2 * HD
QB = 256
FLOOR = -1e29
PEER_ORDER = (1, 6, 7, 2, 3, 4, 5)
LAST_ORDER = ((0, 0), (0, 1), (1, 0), (2, 0), (1, 1), (2, 1))
ONCE = 8


def log2_pieces():
    left, pieces = math.log(2.0), []
    for _ in range(3):
        piece = float(np.asarray(left, jnp.bfloat16))
        pieces.append(piece)
        left -= piece
    return pieces


def partner(me, step):
    other = me
    for bit in (1, 2, 4):
        other = other + bit * (1 - 2 * ((me // bit) % 2)) * ((step // bit) % 2)
    return other


def nt_dot(a, b):
    return lax.dot_general(a, b, (((1,), (1,)), ((), ())), preferred_element_type=jnp.float32)


def fused_kernel(
    n,
    q_ref,
    k_ref,
    v_ref,
    g_ref,
    tissue_ref,
    count_ref,
    grads_ref,
    buf,
    flags,
    key_side,
    query_side,
    key_cols,
    sums,
    res,
    arrive,
    once,
    tissue_here,
    staged,
):
    me = lax.axis_index("seq")
    local = q_ref.shape[0]
    rows = n * local
    pairs = buf.shape[0]
    width = pairs * PAIR
    chip = QB // local
    scaling = 1.0 / math.sqrt(HD)
    peers = [partner(me, step) for step in range(n)]

    def rows_of(device):
        return pl.ds(pl.multiple_of(device * local, local), local)

    def cols_of(device, pair):
        return pl.ds(pl.multiple_of(device * width + pair * PAIR, PAIR), PAIR)

    def remote(src, dst, send, recv, device):
        return pltpu.make_async_remote_copy(
            src_ref=src,
            dst_ref=dst,
            send_sem=send,
            recv_sem=recv,
            device_id={"seq": device},
            device_id_type=pl.DeviceIdType.MESH,
        )

    barrier = pltpu.get_barrier_semaphore()
    for step in PEER_ORDER[1:] + PEER_ORDER[:1]:
        pl.semaphore_signal(
            barrier, inc=1, device_id={"seq": peers[step]}, device_id_type=pl.DeviceIdType.MESH
        )

    flag_send, flag_recv, in_send, out_send, out_recv, own_in, own_out, small = (
        once.at[index] for index in range(ONCE)
    )
    for which in range(2):
        pltpu.make_async_copy((k_ref, v_ref)[which], staged.at[which], once.at[7]).start()
    pl.semaphore_wait(barrier, n - 1)
    pltpu.make_async_copy(staged, staged, once.at[7]).wait()

    ins = (k_ref, v_ref, q_ref, g_ref)

    def send_in(pair, group):
        for step in PEER_ORDER if group else PEER_ORDER[1:] + PEER_ORDER[:1]:
            for which in range(2 * group, 2 * group + 2):
                remote(
                    (staged.at[which] if group == 0 and pair == 0 else ins[which]).at[
                        :, cols_of(peers[step], pair)
                    ],
                    buf.at[pair, which, rows_of(me), :],
                    in_send,
                    arrive.at[pair, 1 + step // chip if group else 0],
                    peers[step],
                ).start()

    send_in(0, 0)
    tissue_copy = pltpu.make_async_copy(tissue_ref, tissue_here, small)
    tissue_copy.start()
    for pair in range(pairs):
        for which in range(4):
            pltpu.make_async_copy(
                ins[which].at[:, cols_of(me, pair)], buf.at[pair, which, rows_of(me), :], own_in
            ).start()
    tissue_copy.wait()
    spot = lax.broadcasted_iota(jnp.int32, flags.shape[1:], 1)
    blocks_here = tissue_here.shape[0]
    tissue = jnp.zeros_like(spot)
    for block in range(blocks_here):
        tissue = jnp.where(spot // (local // blocks_here) == block, tissue_here[block], tissue)
    usable = (me * local + spot < count_ref[0]) & (tissue == 1)
    flags[me] = usable.astype(jnp.float32)
    for step in PEER_ORDER:
        remote(
            flags.at[me, pl.ds(0, 1)], flags.at[me, pl.ds(0, 1)], flag_send, flag_recv, peers[step]
        ).start()
    send_in(0, 1)
    for pair in range(1, pairs):
        send_in(pair, 0)
        send_in(pair, 1)

    def landed(ref, sem):
        remote(ref, ref, in_send, sem, peers[1]).wait_recv()

    def left(ref, sem):
        remote(ref, ref, sem, out_recv, peers[1]).wait_send()

    theirs = pl.ds(0, rows - local)
    mine = buf.at[:, :, pl.ds(0, local), :]
    pltpu.make_async_copy(mine, mine, own_in).wait()
    landed(flags.at[0, pl.ds(0, n - 1)], flag_recv)
    lane = lax.broadcasted_iota(jnp.int32, (local, PAIR), 1)
    residue = lax.broadcasted_iota(jnp.int32, (local, PAIR), 0) % DILATION_STEP
    pieces = log2_pieces()
    piece = jnp.where(lane < 8, pieces[0], jnp.where(lane < 16, pieces[1], pieces[2]))
    same = (lane < 24) & (lane % DILATION_STEP == residue)
    for block in range(n):
        flag = jnp.transpose(jnp.broadcast_to(flags[block, 0:1, :], (local, PAIR)))
        off = (1.0 - flag) * NEG
        side = jnp.where(lane == 24, off, jnp.where(lane == 25, 1.0, jnp.where(same, piece, 0.0)))
        here = pl.ds(block * local, local)
        for pair in range(pairs):
            key_side[pair, here, PAIR:] = side.astype(jnp.bfloat16)
        for head in range(2 * pairs):
            shift = (me * 2 * pairs + head) % DILATION_STEP
            chosen = same & (lane % DILATION_STEP == shift)
            side = jnp.where(
                lane == 24, 1.0, jnp.where(lane == 25, off, jnp.where(chosen, 1.0, 0.0))
            )
            query_side[head, here, :] = side.astype(jnp.bfloat16)

    half = lax.broadcasted_iota(jnp.int32, (QB, PAIR), 1) // HD

    def send_out(pair, which, device):
        remote(
            res.at[pair, which, rows_of(device), :],
            grads_ref.at[which, :, cols_of(me, pair)],
            out_send,
            out_recv,
            device,
        ).start()

    for pair in range(pairs):
        landed(buf.at[pair, pl.ds(0, 2), theirs, :], arrive.at[pair, 0])
        key_side[pair, :, :PAIR] = buf[pair, 0]
        key_cols[...] = jnp.transpose(buf[pair, 0].astype(jnp.float32)).astype(jnp.bfloat16)
        sums[...] = jnp.zeros_like(sums)

        def query_block(index, carry, pair=pair):
            far = (n // chip - index) % (n // chip) if pair == 0 else n // chip - 1 - index
            for count, here in ((chip - 1, far == 0), (chip, far > 0)):

                @pl.when(here)
                def _(count=count):
                    these = pl.ds(0, count * local)
                    landed(buf.at[pair, pl.ds(2, 2), these, :], arrive.at[pair, 1 + far])

            first = partner(me - me % chip, far * chip)
            here = pl.ds(pl.multiple_of(first * local, QB), QB)
            query = buf[pair, 2, here, :].astype(jnp.float32) * scaling
            grad = buf[pair, 3, here, :].astype(jnp.float32)
            columns_out = []
            for side in range(2):
                query_h = jnp.where(half == side, query, 0.0).astype(jnp.bfloat16)
                grad_h = jnp.where(half == side, grad, 0.0).astype(jnp.bfloat16)
                extended = jnp.concatenate(
                    [query_h, query_side[2 * pair + side, here, :]], axis=1
                )
                score = nt_dot(key_side[pair], extended)
                grad_prob = nt_dot(buf[pair, 1], grad_h)
                top = jnp.maximum(jnp.max(score, axis=0, keepdims=True), FLOOR)
                weight = jnp.exp(score - top)
                total = jnp.maximum(jnp.sum(weight, axis=0, keepdims=True), 1.0)
                inverse = 1.0 / total
                delta = jnp.sum(weight * grad_prob, axis=0, keepdims=True) * inverse
                prob = weight * inverse
                dscore = (prob * (grad_prob - delta)).astype(jnp.bfloat16)
                sums[0] += jnp.dot(dscore, query_h, preferred_element_type=jnp.float32)
                sums[1] += jnp.dot(
                    prob.astype(jnp.bfloat16), grad_h, preferred_element_type=jnp.float32
                )
                columns_out.append(
                    jnp.dot(
                        key_cols[side * HD : (side + 1) * HD, :],
                        dscore,
                        preferred_element_type=jnp.float32,
                    )
                )
            grad_query = jnp.transpose(jnp.concatenate(columns_out, axis=0)) * scaling
            res[pair, 0, here, :] = grad_query.astype(jnp.bfloat16)
            for part in range(chip):
                step = far * chip + part

                def leaves(step=step):
                    send_out(pair, 0, partner(me, step))

                if part == 0:
                    pl.when(step > 0)(leaves)
                else:
                    leaves()
            return carry

        lax.fori_loop(0, rows // QB, query_block, 0)
        res[pair, 1] = sums[0].astype(jnp.bfloat16)
        res[pair, 2] = sums[1].astype(jnp.bfloat16)
        send_out(pair, pl.ds(1, 2), peers[1])
        here_chip = me // 2
        first = here_chip + 3 * ((3 - here_chip) // 3)
        second = 3 - 2 * (first // 3)
        order = (first, second, 6 - first - second)
        for place, core in LAST_ORDER:
            step = 2 * order[place] + core + (me % 2) * (1 - 2 * core)
            send_out(pair, pl.ds(1, 2), partner(me, step))
        pltpu.make_async_copy(
            res.at[pair, :, rows_of(me), :], grads_ref.at[:, :, cols_of(me, pair)], own_out
        ).start()
    left(flags.at[0, pl.ds(0, n - 1)], flag_send)
    left(buf.at[:, :, theirs, :], in_send)
    mine = res.at[:, :, pl.ds(0, local), :]
    pltpu.make_async_copy(mine, mine, own_out).wait()
    left(res.at[:, :, theirs, :], out_send)
    landed(res.at[:, :, theirs, :], out_recv)


def write_kernel(grads_ref, dq_ref, dk_ref, dv_ref, sem):
    copies = [
        pltpu.make_async_copy(grads_ref.at[which], out, sem.at[0])
        for which, out in enumerate((dq_ref, dk_ref, dv_ref))
    ]
    for copy in copies:
        copy.start()
    for copy in copies:
        copy.wait()


def on_device_fused(n, queries, keys, values, out_grad, tissue, valid_count):
    local, features = queries.shape
    rows = n * local
    pairs = features // n // PAIR
    hbm = pl.BlockSpec(memory_space=pltpu.HBM)
    vmem = pl.BlockSpec(memory_space=pltpu.VMEM)
    smem = pl.BlockSpec(memory_space=pltpu.SMEM)
    dma = pltpu.SemaphoreType.DMA
    grads = pl.pallas_call(
        functools.partial(fused_kernel, n),
        out_shape=pltpu.VMEM((3, local, features), jnp.bfloat16),
        in_specs=[hbm] * 5 + [smem],
        out_specs=vmem,
        scratch_shapes=[
            pltpu.VMEM((pairs, 4, rows, PAIR), jnp.bfloat16),
            pltpu.VMEM((n, 8, local), jnp.float32),
            pltpu.VMEM((pairs, rows, 2 * PAIR), jnp.bfloat16),
            pltpu.VMEM((2 * pairs, rows, PAIR), jnp.bfloat16),
            pltpu.VMEM((PAIR, rows), jnp.bfloat16),
            pltpu.VMEM((2, rows, PAIR), jnp.float32),
            pltpu.VMEM((pairs, 3, rows, PAIR), jnp.bfloat16),
            dma((pairs, 1 + rows // QB)),
            dma((ONCE,)),
            pltpu.SMEM(tissue.shape, jnp.int32),
            pltpu.VMEM((2, local, features), jnp.bfloat16),
        ],
        compiler_params=pltpu.CompilerParams(
            collective_id=0, has_side_effects=True, vmem_limit_bytes=48 * 2**20
        ),
        name="attention_backward",
    )(
        *(
            pltpu.with_memory_space_constraint(entry, pltpu.HBM)
            for entry in (queries, keys, values, out_grad, tissue)
        ),
        valid_count,
    )
    return tuple(
        pl.pallas_call(
            write_kernel,
            out_shape=[jax.ShapeDtypeStruct((local, features), jnp.bfloat16)] * 3,
            in_specs=[vmem],
            out_specs=[hbm] * 3,
            scratch_shapes=[dma((1,))],
            compiler_params=pltpu.CompilerParams(vmem_limit_bytes=4 * 2**20),
            name="write_gradients",
        )(grads)
    )


def solution(mesh):
    in_specs = (
        P(("slide", "seq"), None),
        P(("slide", "seq"), None),
        P(("slide", "seq"), None),
        P(("slide", "seq"), None),
        P(("slide", "seq")),
        P("slide"),
    )
    out_specs = (P(("slide", "seq"), None), P(("slide", "seq"), None), P(("slide", "seq"), None))
    n = mesh.shape["seq"]

    def body(queries, keys, values, out_grad, tissue, valid_count):
        arguments = (queries, keys, values, out_grad, tissue, valid_count)
        local, features = queries.shape
        if n == 8 and local == PAIR and n * local == SEG and features % (n * PAIR) == 0:
            return on_device_fused(n, *arguments)
        return on_device(*arguments)

    return jax.shard_map(
        body, mesh=mesh, in_specs=in_specs, out_specs=out_specs, check_vma=False
    )
```
